512 devices in a mesh: dp: 16 (over z), seq: 8 (over x, core), index: 4 (over y).
Axes of the slice: x: 4, y: 4, z: 16, core: 2. Of those that a mesh axis runs over, the one named last changes fastest.
Arguments:
- hidden: bfloat16 [16, 2048, 2048], P('dp', 'seq'), may hold values from -32 to 32
- proj_weight: bfloat16 [4, 2048, 1536], P(None, 'dp', 'index')
- stretch_lengths: int32 [16, 32], P('dp'), may hold values from 1 to 512, 2048 in all within a row
- shard_of: int32 [16, 32, 1], P('dp', 'seq'), may hold values from 0 to 3; in each aligned block of 4 rows (0 to 3, 4 to 7, ..., all dimensions but the last counted through in order) at most 2 rows name the same one
Outputs:
- layer_out: bfloat16 [16, 2048, 2048], P('dp', 'seq', 'index')
- shelf: float32 [16, 8, 4, 2, 2048], P('dp', 'seq', 'index')
The draws below stay inside these ranges and needn't reach their ends.
Inputs may be any that keep to these rules, and one draw needn't show every extreme that they name: `stretch_lengths`: the 32 lengths of a manual sum to 2048; the largest is 512. `shard_of`: in each aligned block of 4 rows of a manual no shard is named more than 2 times, a bound that some block reaches.
All inputs are finite; a program needn't handle non-finite values.
Results may differ from the reference program's by a relative error of at most 0.01.
Values may be sent and summed in bfloat16 or wider, within the bound.
A program may use at most 64 MiB of HBM per device.

```python
import math
import jax
import jax.numpy as jnp
import numpy as np
from jax import lax

D = 2048
HEADS = 24
HD = 64
HALF_WIN = 256
CH_MOST = 512
STRETCHES = 32
MANUALS = 16
LENGTH = 2048
BLOCKS = 8
HEAD_GROUPS = 4
CH_DEV = 4
CAP = 2


def draw_hidden(key, part):
    shape = (MANUALS, LENGTH, D)
    first = jax.random.fold_in(key, 0)
    values = jnp.clip(jax.random.normal(first, shape, jnp.float32), -6.0, 6.0)
    return jnp.clip(values, -32.0, 32.0).astype(jnp.bfloat16)


def draw_proj_weight(key, part):
    shape = (4, D, HEADS * HD)
    first = jax.random.fold_in(key, 0)
    values = jnp.clip(jax.random.normal(first, shape, jnp.float32), -4.0, 4.0)
    return (values * D ** (-0.5)).astype(jnp.bfloat16)


def profile(count, total, bound, lean):
    portions = [(1 << 20) // math.isqrt(rank ** lean) + 1 for rank in range(2, count + 1)]
    surplus, holding = total - bound - (count - 1), [1] * (count - 1)
    while surplus > 0:
        movable = [i for i in range(count - 1) if holding[i] < bound]
        mass, left = sum([portions[i] for i in movable]), surplus
        for i in movable:
            addition = min(bound - holding[i], max(1, left * portions[i] // mass), surplus)
            holding[i] = holding[i] + addition
            surplus = surplus - addition
    return np.array([bound] + holding)


def ragged(stream_key, amount, total, limit, lean):
    if amount == 2:
        one = jax.random.randint(stream_key, (), max(1, total - limit), min(limit, total - 1) + 1)
        return jnp.stack([one, total - one])
    sizes = jnp.asarray(profile(amount, total, limit, lean), jnp.int32)
    twos = (amount - 1) // 2
    giver, taker = sizes[1:1 + 2 * twos:2], sizes[2:2 + 2 * twos:2]
    margin = jnp.minimum(giver - 1, limit - taker)
    moved = jax.random.randint(jax.random.fold_in(stream_key, 1), (twos,), 0, 1 << 20) % (margin + 1)
    sizes = sizes.at[1:1 + 2 * twos:2].set(giver - moved).at[2:2 + 2 * twos:2].set(taker + moved)
    return sizes[jax.random.permutation(jax.random.fold_in(stream_key, 2), amount)]


def shared_out(stream_key, own, number, rows, amount, top, reach, lean):
    order = jax.random.permutation(stream_key, amount)
    packed, usual = portions_of(amount, rows * top, reach, lean, True), portions_of(amount, rows * top, reach, lean, False)
    places = jnp.arange(amount)

    def named(sizes, offset_by):
        used = int((sizes > 0).sum())
        fixed = max(1, used // 4)
        moved = fixed + (places - fixed + offset_by * (used - fixed)) % max(1, amount - fixed)
        return jnp.zeros((amount,), jnp.int32).at[order[jnp.where(places < fixed, places, moved)]].set(jnp.asarray(sizes, jnp.int32))

    sizes = jnp.where(number % 4 == 0, named(packed, number // 4), named(usual, number - number // 4 - 1))
    mixed = jax.random.permutation(jax.random.fold_in(own, 3), amount)
    donor, taker = mixed[0:amount // 2 * 2:2], mixed[1:amount // 2 * 2:2]
    room = jnp.minimum(sizes[donor] - 1, reach - sizes[taker]) // 2
    room = jnp.where((donor == order[0]) | (taker == order[0]) | (sizes[taker] == 0), 0, jnp.maximum(room, 0))
    moved = jax.random.randint(jax.random.fold_in(own, 4), (amount // 2,), 0, 1 << 20) % (room + 1)
    sizes = sizes.at[donor].add(-moved).at[taker].add(moved)
    items = jnp.searchsorted(jnp.cumsum(sizes), jnp.arange(rows * top), side="right").astype(jnp.int32)
    table = items.reshape(top, rows).T
    table = table[jax.random.permutation(jax.random.fold_in(own, 1), rows)]
    offset_by = jax.random.randint(jax.random.fold_in(own, 2), (rows, 1), 0, top)
    return jnp.take_along_axis(table, (jnp.arange(top)[None, :] + offset_by) % top, axis=1)


def portions_of(number_of, total, reach, skew, full):
    weights = [(1 << 20) // math.isqrt(rank ** skew) + 1 for rank in range(1, number_of + 1)]
    largest = reach if full else min(reach, max(-(-total // number_of), total * weights[0] // sum(weights)))
    least = 1 if total - largest >= number_of - 1 else 0
    counts, surplus = [largest] + [least] * (number_of - 1), total - largest - least * (number_of - 1)
    while surplus > 0:
        movable = [i for i in range(1, number_of) if counts[i] < largest] or [i for i in range(1, number_of) if counts[i] < reach]
        mass, left = sum([weights[i] for i in movable]), surplus
        for i in movable:
            more = min(reach - counts[i], max(1, left * weights[i] // mass), surplus)
            counts[i] = counts[i] + more
            surplus = surplus - more
    return np.array(counts)


def setup_inputs(seed: int = 0) -> dict:
    keys = jax.random.split(jax.random.key(seed), 5)
    hidden = draw_hidden(jax.random.fold_in(keys[4], 71), 0)
    proj_weight = draw_proj_weight(jax.random.fold_in(keys[4], 71), 0)
    stretch_lengths = jax.vmap(lambda own: ragged(own, STRETCHES, LENGTH, CH_MOST, 2))(jax.random.split(keys[2], MANUALS)).reshape((MANUALS, STRETCHES)).astype(jnp.int32)
    shard_of_keys = jax.random.split(jax.random.fold_in(keys[3], 1), MANUALS * STRETCHES // CH_DEV)
    shard_of_turns = jax.random.permutation(jax.random.fold_in(keys[3], 3), MANUALS * STRETCHES // CH_DEV)
    shard_of = jax.vmap(lambda own, number: shared_out(jax.random.fold_in(keys[3], 2), own, number, CH_DEV, HEAD_GROUPS, 1, CAP, 2))(shard_of_keys, shard_of_turns).reshape((MANUALS, STRETCHES, 1))
    return dict(hidden=hidden, proj_weight=proj_weight, stretch_lengths=stretch_lengths, shard_of=shard_of)


def rotate(values_in, positions):
    half_dim = HD // 2
    freqs = 10000.0 ** (-2.0 * jnp.arange(half_dim, dtype=jnp.float32) / HD)
    angles = positions.astype(jnp.float32)[:, None] * freqs[None, :]
    cosine = jnp.cos(angles)[:, None, :]
    sine = jnp.sin(angles)[:, None, :]
    first = values_in[..., :half_dim]
    second = values_in[..., half_dim:]
    return jnp.concatenate([first * cosine - second * sine, second * cosine + first * sine], -1)

def window_heads(queries, key_rows, value_rows, visible):
    scale = HD ** (-0.5)

    def one_head(items):
        query_head, key_head, value_head = items
        scores = jnp.dot(query_head, key_head.T, preferred_element_type=jnp.float32) * scale
        scores = jnp.where(visible, scores, -1e+30)
        maxima = lax.optimization_barrier(jnp.max(scores, -1, keepdims=True))
        expo = jnp.exp(scores - maxima)
        weights = (expo / lax.optimization_barrier(jnp.sum(expo, -1, keepdims=True))).astype(jnp.bfloat16)
        return jnp.dot(weights, value_head, preferred_element_type=jnp.float32).astype(jnp.bfloat16)
    context = lax.map(one_head, (jnp.moveaxis(queries, 1, 0), jnp.moveaxis(key_rows, 1, 0), jnp.moveaxis(value_rows, 1, 0)))
    return jnp.moveaxis(context, 0, 1)

def attend_manual(queries, key_rows, value_rows):
    block = min(512, LENGTH)
    count = LENGTH // block
    padding = ((HALF_WIN, HALF_WIN), (0, 0), (0, 0))
    key_pad = jnp.pad(key_rows, padding)
    value_pad = jnp.pad(value_rows, padding)
    span = block + 2 * HALF_WIN

    def one_block(index_block):
        offset = index_block * block
        query_part = lax.dynamic_slice_in_dim(queries, offset, block, 0)
        key_part = lax.dynamic_slice_in_dim(key_pad, offset, span, 0)
        value_part = lax.dynamic_slice_in_dim(value_pad, offset, span, 0)
        query_pos = offset + jnp.arange(block, dtype=jnp.int32)
        key_pos = offset - HALF_WIN + jnp.arange(span, dtype=jnp.int32)
        visible = (jnp.abs(key_pos[None, :] - query_pos[:, None]) <= HALF_WIN) & (key_pos[None, :] >= 0) & (key_pos[None, :] < LENGTH)
        return window_heads(query_part, key_part, value_part, visible)
    blocks_out = lax.map(one_block, jnp.arange(count, dtype=jnp.int32))
    return blocks_out.reshape(LENGTH, HEADS, HD)

def reference(hidden, proj_weight, stretch_lengths, shard_of):
    width = HEADS // HEAD_GROUPS * HD

    def one_manual(items):
        states, lengths, shards = items
        positions = jnp.arange(LENGTH, dtype=jnp.int32)
        projected = [jnp.dot(states, proj_weight[j], preferred_element_type=jnp.float32) for j in range(3)]
        queries = rotate(projected[0].reshape(LENGTH, HEADS, HD), positions).astype(jnp.bfloat16)
        key_rows = rotate(projected[1].reshape(LENGTH, HEADS, HD), positions).astype(jnp.bfloat16)
        value_rows = projected[2].reshape(LENGTH, HEADS, HD).astype(jnp.bfloat16)
        context = attend_manual(queries, key_rows, value_rows).reshape(LENGTH, HEADS * HD)
        running = states.astype(jnp.float32)
        for group_index in range(HEAD_GROUPS):
            cols = slice(group_index * width, (group_index + 1) * width)
            partial_value = jnp.dot(context[:, cols], proj_weight[3][:, cols].T, preferred_element_type=jnp.float32).astype(jnp.bfloat16)
            running = running + partial_value.astype(jnp.float32)
        layer = running.astype(jnp.bfloat16)
        ends = jnp.cumsum(lengths, dtype=jnp.int32)
        starts = ends - lengths
        row_ids = jnp.arange(STRETCHES, dtype=jnp.int32)
        order = (row_ids % CH_DEV * BLOCKS + row_ids // CH_DEV).astype(jnp.int32)
        row_starts = starts[order]
        row_ends = ends[order]
        member = ((positions[None, :] >= row_starts[:, None]) & (positions[None, :] < row_ends[:, None])).astype(jnp.bfloat16)
        pooled = jnp.dot(member, layer, preferred_element_type=jnp.float32)
        embedded = pooled * lax.rsqrt(lax.optimization_barrier(jnp.mean(pooled * pooled, -1, keepdims=True)) + 1e-06)
        shard_ids = shards[:, 0].astype(jnp.int32)
        block_ids = row_ids // CH_DEV
        earlier = (shard_ids[:, None] == shard_ids[None, :]) & (block_ids[:, None] == block_ids[None, :]) & (row_ids[None, :] < row_ids[:, None])
        slot_rank = lax.optimization_barrier(jnp.sum(earlier.astype(jnp.int32), 1)).astype(jnp.int32)
        place = (block_ids * HEAD_GROUPS + shard_ids) * CAP + slot_rank
        targets = jnp.arange(BLOCKS * HEAD_GROUPS * CAP, dtype=jnp.int32)
        onehot = (place[None, :] == targets[:, None]).astype(jnp.float32)
        shelf_rows = jnp.dot(onehot, embedded, precision=lax.Precision.HIGHEST)
        return (layer, shelf_rows.reshape(BLOCKS, HEAD_GROUPS, CAP, D))
    layer_out, shelf = lax.map(one_manual, (hidden, stretch_lengths, shard_of))
    return (layer_out, shelf)
```

```python
import functools

import jax
import jax.numpy as jnp
from jax import lax
from jax.experimental import pallas as pl
from jax.experimental.pallas import tpu as pltpu
from jax.sharding import PartitionSpec as P

D = 2048
HD = 64
HALF_WIN = 256
MESH = pl.DeviceIdType.MESH
VMEM = pltpu.VMEM


def rope_tables(positions, lanes):
    lane = jnp.arange(lanes, dtype=jnp.int32) % HD
    half = HD // 2
    freqs = 10000.0 ** (-2.0 * (lane % half).astype(jnp.float32) / HD)
    angles = positions.astype(jnp.float32)[:, None] * freqs[None, :]
    sign = jnp.where(lane < half, -1.0, 1.0).astype(jnp.float32)
    return jnp.cos(angles), jnp.sin(angles) * sign[None, :]


def gather_kernel(x_ref, w_ref, cos_ref, sin_ref, q_ref, k_ref, v_ref, o_ref,
                  w_all, acc, local_sem, zs, zr, xs, xr, ps, pr):
    nz = lax.axis_size("dp")
    ns = lax.axis_size("seq")
    z = lax.axis_index("dp")
    s = lax.axis_index("seq")
    half = nz // 2
    rows = w_ref.shape[1]
    pieces = w_ref.shape[0]
    core = lax.rem(s, 2)
    par = lax.rem(s // 2, 2)
    partner = s + 1 - 2 * core
    up = {"dp": lax.rem(z + 1, nz)}
    down = {"dp": lax.rem(z + nz - 1, nz)}
    right = {"seq": lax.rem(s + 2, ns)}
    left = {"seq": lax.rem(s + ns - 2, ns)}
    mate = {"seq": partner}

    barrier = pltpu.get_barrier_semaphore()
    for peer in (up, down, right, left, mate):
        pl.semaphore_signal(barrier, inc=1, device_id=peer, device_id_type=MESH)
    pl.semaphore_wait(barrier, 5)

    part = rows // 4
    sub = part // 2
    mine = pl.multiple_of(rows // 2 * par + part * core, 16)
    other = pl.multiple_of(rows // 2 * (1 - par) + part * core, 16)

    def remote(src, dst, send, recv, device):
        return pltpu.make_async_remote_copy(src_ref=src, dst_ref=dst, send_sem=send, recv_sem=recv,
                                            device_id=device, device_id_type=MESH)

    def z_copy(g, o, slot, device, first=False):
        ref = w_all.at[o, g, pl.ds(mine, part)]
        src = w_ref.at[g, pl.ds(mine, part)] if first else ref
        return remote(src, ref, zs.at[g, slot], zr.at[g, o], device)

    def z_wait(g, o):
        z_copy(g, o, o, up).wait_recv()

    def x_copy(o, which):
        ref = w_all.at[o, :, pl.ds(mine + which * sub, sub)]
        return remote(ref, ref, xs.at[which, o], xr.at[which, o], (right, left)[which])

    def x_wait(o, which):
        ref = w_all.at[o, :, pl.ds(other + which * sub, sub)]
        remote(ref, ref, xs.at[which, o], xr.at[which, o], right).wait_recv()

    def p_copy(o, which):
        start = (mine, other)[which]
        ref = w_all.at[o, :, pl.ds(start, part)]
        return remote(ref, ref, ps.at[which, o], pr.at[which, o], mate)

    def p_wait(o, which):
        start = pl.multiple_of(rows // 2 * ((par, 1 - par)[which]) + part * (1 - core), 16)
        ref = w_all.at[o, :, pl.ds(start, part)]
        remote(ref, ref, ps.at[which, o], pr.at[which, o], mate).wait_recv()

    def minus(k):
        return lax.rem(z + nz - k, nz)

    def plus(k):
        return lax.rem(z + k, nz)

    for g in range(pieces):
        z_copy(g, z, z, up, True).start()
        z_copy(g, z, plus(half), down, True).start()
    own = pltpu.make_async_copy(w_ref, w_all.at[z], local_sem)
    own.start()
    acc[...] = jnp.zeros_like(acc)
    own.wait()

    def arrive(o, k, last, device):
        for g in range(pieces):
            z_wait(g, o)

            @pl.when(k < last)
            def _():
                z_copy(g, o, o, device).start()
        for which in range(2):
            x_copy(o, which).start()
        p_copy(o, 0).start()

    def cross(o):
        for which in range(2):
            x_wait(o, which)
        p_copy(o, 1).start()

    def multiply(a, b):
        cols_a = pl.ds(pl.multiple_of(a * rows, 128), rows)
        cols_b = pl.ds(pl.multiple_of(b * rows, 128), rows)
        lhs = jnp.concatenate([x_ref[:, cols_a], x_ref[:, cols_b]], axis=1)
        for j in range(3):
            rhs = jnp.concatenate([w_all[a, j], w_all[b, j]], axis=0)
            acc[j] += jnp.dot(lhs, rhs, preferred_element_type=jnp.float32)

    def settle(o):
        p_wait(o, 0)
        p_wait(o, 1)

    def step(k, carry):
        arrive(minus(k), k, half, up)

        @pl.when(k < half)
        def _():
            arrive(plus(k), k, half - 1, down)

        @pl.when(k >= 2)
        def _():
            cross(minus(k - 1))
            cross(plus(k - 1))

        @pl.when(k >= 3)
        def _():
            a, b = minus(k - 2), plus(k - 2)
            settle(a)
            settle(b)
            multiply(a, b)

        return carry

    lax.fori_loop(1, half + 1, step, 0)
    cross(minus(half))
    settle(minus(half - 1))
    settle(plus(half - 1))
    multiply(minus(half - 1), plus(half - 1))
    settle(minus(half))
    multiply(z, minus(half))

    width = q_ref.shape[1]
    lane = lax.broadcasted_iota(jnp.int32, (q_ref.shape[0], 128), 1)
    lower = lax.rem(lane, HD) < HD // 2
    for j, ref in ((0, q_ref), (1, k_ref)):
        for start in range(0, width, 128):
            value = acc[j, :, start:start + 128]
            swapped = jnp.where(lower, pltpu.roll(value, 128 - HD // 2, 1), pltpu.roll(value, HD // 2, 1))
            ref[:, start:start + 128] = (value * cos_ref[...] + swapped * sin_ref[...]).astype(jnp.bfloat16)
    v_ref[...] = acc[2].astype(jnp.bfloat16)
    o_ref[...] = w_all[:, 3]

    def finish(k, carry):
        a, b = minus(k), plus(k)
        for g in range(pieces):
            z_copy(g, a, a, up).wait_send()

            @pl.when(k < half - 1)
            def _():
                z_copy(g, b, jnp.where(k == 0, plus(half), b), down).wait_send()
        return carry

    lax.fori_loop(0, half, finish, 0)

    def finish_cross(k, carry):
        o = plus(k)
        for which in range(2):
            x_copy(o, which).wait_send()
            p_copy(o, which).wait_send()
        return carry

    lax.fori_loop(1, nz, finish_cross, 0)


def gathered_projection(states, weights, cosine, sine):
    tokens = states.shape[0]
    pieces, rows, width = weights.shape
    nz = lax.axis_size("dp")
    out = jax.ShapeDtypeStruct((tokens, width), jnp.bfloat16)
    dma = pltpu.SemaphoreType.DMA
    return pl.pallas_call(
        gather_kernel,
        out_shape=(out, out, out, jax.ShapeDtypeStruct((nz, rows, width), jnp.bfloat16)),
        in_specs=[pl.BlockSpec(memory_space=VMEM)] * 4,
        out_specs=[pl.BlockSpec(memory_space=VMEM)] * 4,
        scratch_shapes=[
            VMEM((nz, pieces, rows, width), jnp.bfloat16),
            VMEM((3, tokens, width), jnp.float32),
            dma(()),
            dma((pieces, nz)), dma((pieces, nz)),
            dma((2, nz)), dma((2, nz)), dma((2, nz)), dma((2, nz)),
        ],
        compiler_params=pltpu.CompilerParams(collective_id=0, has_side_effects=True),
    )(states, weights, cosine, sine)


def with_halo(cells, sides, width):
    for axis, dim in sides:
        count = lax.axis_size(axis)
        ends = count - 1
        head = lax.slice_in_dim(cells, 0, width, axis=dim)
        tail = lax.slice_in_dim(cells, cells.shape[dim] - width, cells.shape[dim], axis=dim)
        cells = jnp.concatenate(
            [
                lax.ppermute(tail, axis, [(i, (i + 1) % count) for i in range(ends)]),
                cells,
                lax.ppermute(head, axis, [((i + 1) % count, i) for i in range(ends)]),
            ],
            axis=dim,
        )
    return cells


def window_heads(queries, key_rows, value_rows, visible):
    scale = HD ** (-0.5)

    def one_head(items):
        query_head, key_head, value_head = items
        scores = jnp.dot(query_head, key_head.T, preferred_element_type=jnp.float32) * scale
        scores = jnp.where(visible, scores, -1e30)
        maxima = jnp.max(scores, -1, keepdims=True)
        expo = jnp.exp(scores - maxima)
        weights = (expo / jnp.sum(expo, -1, keepdims=True)).astype(jnp.bfloat16)
        return jnp.dot(weights, value_head, preferred_element_type=jnp.float32).astype(jnp.bfloat16)

    context = lax.map(
        one_head,
        (jnp.moveaxis(queries, 1, 0), jnp.moveaxis(key_rows, 1, 0), jnp.moveaxis(value_rows, 1, 0)),
    )
    return jnp.moveaxis(context, 0, 1)


def body(hidden, proj_weight, stretch_lengths, shard_of):
    states = hidden[0]
    tokens_here = states.shape[0]
    width = proj_weight.shape[2]
    heads_here = width // HD
    seq_index = lax.axis_index("seq")
    group_index = lax.axis_index("index")
    seq_count = lax.axis_size("seq")
    index_count = lax.axis_size("index")
    total_length = tokens_here * seq_count
    positions = seq_index * tokens_here + jnp.arange(tokens_here, dtype=jnp.int32)
    cosine, sine = rope_tables(positions, 128)
    queries, keys, value_rows, out_rows = gathered_projection(states, proj_weight, cosine, sine)
    out_rows_full = out_rows.reshape(-1, width)
    queries = queries.reshape(tokens_here, heads_here, HD)
    stacked = jnp.stack([keys, value_rows])
    padded = with_halo(stacked, (("seq", 1),), HALF_WIN)
    span = tokens_here + 2 * HALF_WIN
    key_part = padded[0, 0:span].reshape(span, heads_here, HD)
    value_part = padded[1, 0:span].reshape(span, heads_here, HD)
    key_pos = seq_index * tokens_here + 0 - HALF_WIN + jnp.arange(span, dtype=jnp.int32)
    visible = (
        (jnp.abs(key_pos[None, :] - positions[:, None]) <= HALF_WIN)
        & (key_pos[None, :] >= 0)
        & (key_pos[None, :] < total_length)
    )
    context_parts = window_heads(queries, key_part, value_part, visible).reshape(tokens_here, width)
    partial_value = lax.dot_general(
        context_parts, out_rows_full, (((1,), (1,)), ((), ())), preferred_element_type=jnp.float32
    )
    lengths = stretch_lengths[0]
    stretch_count = lengths.shape[0]
    per_block = stretch_count // seq_count
    ends = jnp.cumsum(lengths, dtype=jnp.int32)
    starts = ends - lengths
    row_ids = jnp.arange(stretch_count, dtype=jnp.int32)
    order = row_ids % per_block * seq_count + row_ids // per_block
    row_starts = starts[order]
    row_ends = ends[order]
    member = (
        (positions[None, :] >= row_starts[:, None]) & (positions[None, :] < row_ends[:, None])
    ).astype(jnp.bfloat16)
    shard_ids = shard_of[0, :, 0]
    local_rows = jnp.arange(per_block, dtype=jnp.int32)
    earlier = (shard_ids[:, None] == shard_ids[None, :]) & (
        local_rows[None, :] < local_rows[:, None]
    )
    slot_rank = jnp.sum(earlier.astype(jnp.int32), 1)
    capacity = per_block // 2
    slot_ids = jnp.arange(capacity, dtype=jnp.int32)
    quarter = D // index_count
    summed = lax.psum_scatter(
        partial_value.astype(jnp.bfloat16), "index", scatter_dimension=1, tiled=True
    ).astype(jnp.float32)
    own_states = lax.dynamic_slice_in_dim(states, group_index * quarter, quarter, 1)
    layer = (own_states.astype(jnp.float32) + summed).astype(jnp.bfloat16)
    partial_pool = jnp.dot(member, layer, preferred_element_type=jnp.float32)
    pooled = lax.psum_scatter(
        partial_pool.astype(jnp.bfloat16), "seq", scatter_dimension=0, tiled=True
    ).astype(jnp.float32)
    shard_range = jnp.arange(index_count, dtype=jnp.int32)
    routing = (
        (shard_ids[None, None, :] == shard_range[:, None, None])
        & (slot_rank[None, None, :] == slot_ids[None, :, None])
    ).astype(jnp.float32)
    outgoing = jnp.einsum("rkc,cf->rkf", routing, pooled, precision=lax.Precision.HIGHEST)
    arrived = lax.all_to_all(outgoing, "index", split_axis=0, concat_axis=2, tiled=True)[0]
    shelf_rows = arrived * lax.rsqrt(jnp.mean(arrived * arrived, -1, keepdims=True) + 1e-06)
    return (layer[None], shelf_rows[None, None, None])


def solution(mesh):
    in_specs = (P("dp", "seq", None), P(None, "dp", "index"), P("dp", None), P("dp", "seq", None))
    out_specs = (P("dp", "seq", "index"), P("dp", "seq", "index", None, None))
    return jax.shard_map(body, mesh=mesh, in_specs=in_specs, out_specs=out_specs, check_vma=False)
```

```python
import functools

import jax
import jax.numpy as jnp
from jax import lax
from jax.experimental import pallas as pl
from jax.experimental.pallas import tpu as pltpu
from jax.sharding import PartitionSpec as P

D = 2048
HD = 64
HALF_WIN = 256
MESH = pl.DeviceIdType.MESH
VMEM = pltpu.VMEM


def rope_tables(positions, lanes):
    lane = jnp.arange(lanes, dtype=jnp.int32) % HD
    half = HD // 2
    freqs = 10000.0 ** (-2.0 * (lane % half).astype(jnp.float32) / HD)
    angles = positions.astype(jnp.float32)[:, None] * freqs[None, :]
    sign = jnp.where(lane < half, -1.0, 1.0).astype(jnp.float32)
    return jnp.cos(angles), jnp.sin(angles) * sign[None, :]


def gather_kernel(x_ref, w_ref, cos_ref, sin_ref, q_ref, kv_ref, o_ref,
                  w_all, acc, local_sem, zs, zr, xs, xr, ps, pr):
    nz = lax.axis_size("dp")
    ns = lax.axis_size("seq")
    z = lax.axis_index("dp")
    s = lax.axis_index("seq")
    half = nz // 2
    rows = w_ref.shape[1]
    pieces = w_ref.shape[0]
    core = lax.rem(s, 2)
    par = lax.rem(s // 2, 2)
    partner = s + 1 - 2 * core
    up = {"dp": lax.rem(z + 1, nz)}
    down = {"dp": lax.rem(z + nz - 1, nz)}
    right = {"seq": lax.rem(s + 2, ns)}
    left = {"seq": lax.rem(s + ns - 2, ns)}
    mate = {"seq": partner}

    barrier = pltpu.get_barrier_semaphore()
    for peer in (up, down, right, left, mate):
        pl.semaphore_signal(barrier, inc=1, device_id=peer, device_id_type=MESH)
    pl.semaphore_wait(barrier, 5)

    part = rows // 4
    sub = part // 2
    mine = pl.multiple_of(rows // 2 * par + part * core, 16)
    other = pl.multiple_of(rows // 2 * (1 - par) + part * core, 16)

    def remote(src, dst, send, recv, device):
        return pltpu.make_async_remote_copy(src_ref=src, dst_ref=dst, send_sem=send, recv_sem=recv,
                                            device_id=device, device_id_type=MESH)

    def z_copy(g, o, slot, device, first=False):
        ref = w_all.at[o, g, pl.ds(mine, part)]
        src = w_ref.at[g, pl.ds(mine, part)] if first else ref
        return remote(src, ref, zs.at[g, slot], zr.at[g, o], device)

    def z_wait(g, o):
        z_copy(g, o, o, up).wait_recv()

    def x_copy(o, which):
        ref = w_all.at[o, :, pl.ds(mine + which * sub, sub)]
        return remote(ref, ref, xs.at[which, o], xr.at[which, o], (right, left)[which])

    def x_wait(o, which):
        ref = w_all.at[o, :, pl.ds(other + which * sub, sub)]
        remote(ref, ref, xs.at[which, o], xr.at[which, o], right).wait_recv()

    def p_copy(o, which):
        start = (mine, other)[which]
        ref = w_all.at[o, :, pl.ds(start, part)]
        return remote(ref, ref, ps.at[which, o], pr.at[which, o], mate)

    def p_wait(o, which):
        start = pl.multiple_of(rows // 2 * ((par, 1 - par)[which]) + part * (1 - core), 16)
        ref = w_all.at[o, :, pl.ds(start, part)]
        remote(ref, ref, ps.at[which, o], pr.at[which, o], mate).wait_recv()

    def minus(k):
        return lax.rem(z + nz - k, nz)

    def plus(k):
        return lax.rem(z + k, nz)

    for g in range(pieces):
        z_copy(g, z, z, up, True).start()
        z_copy(g, z, plus(half), down, True).start()
    own = pltpu.make_async_copy(w_ref, w_all.at[z], local_sem)
    own.start()
    acc[...] = jnp.zeros_like(acc)
    own.wait()

    def arrive(o, k, last, device):
        for g in range(pieces):
            z_wait(g, o)

            @pl.when(k < last)
            def _():
                z_copy(g, o, o, device).start()
        for which in range(2):
            x_copy(o, which).start()
        p_copy(o, 0).start()

    def cross(o):
        for which in range(2):
            x_wait(o, which)
        p_copy(o, 1).start()

    def multiply(a, b):
        cols_a = pl.ds(pl.multiple_of(a * rows, 128), rows)
        cols_b = pl.ds(pl.multiple_of(b * rows, 128), rows)
        lhs = jnp.concatenate([x_ref[:, cols_a], x_ref[:, cols_b]], axis=1)
        for j in range(3):
            rhs = jnp.concatenate([w_all[a, j], w_all[b, j]], axis=0)
            acc[j] += jnp.dot(lhs, rhs, preferred_element_type=jnp.float32)

    def settle(o):
        p_wait(o, 0)
        p_wait(o, 1)

    def step(k, carry):
        arrive(minus(k), k, half, up)

        @pl.when(k < half)
        def _():
            arrive(plus(k), k, half - 1, down)

        @pl.when(k >= 2)
        def _():
            cross(minus(k - 1))
            cross(plus(k - 1))

        @pl.when(k >= 3)
        def _():
            a, b = minus(k - 2), plus(k - 2)
            settle(a)
            settle(b)
            multiply(a, b)

        return carry

    lax.fori_loop(1, half + 1, step, 0)
    cross(minus(half))
    settle(minus(half - 1))
    settle(plus(half - 1))
    multiply(minus(half - 1), plus(half - 1))
    settle(minus(half))
    multiply(z, minus(half))

    width = q_ref.shape[1]
    lane = lax.broadcasted_iota(jnp.int32, (q_ref.shape[0], 128), 1)
    lower = lax.rem(lane, HD) < HD // 2
    for j, ref, scale in ((0, q_ref, HD ** -0.5), (1, kv_ref.at[0], 1.0)):
        for start in range(0, width, 128):
            value = acc[j, :, start:start + 128]
            swapped = jnp.where(lower, pltpu.roll(value, 128 - HD // 2, 1), pltpu.roll(value, HD // 2, 1))
            ref[:, start:start + 128] = ((value * cos_ref[...] + swapped * sin_ref[...]) * scale).astype(jnp.bfloat16)
    kv_ref[1] = acc[2].astype(jnp.bfloat16)
    o_ref[...] = w_all[:, 3]

    def finish(k, carry):
        a, b = minus(k), plus(k)
        for g in range(pieces):
            z_copy(g, a, a, up).wait_send()

            @pl.when(k < half - 1)
            def _():
                z_copy(g, b, jnp.where(k == 0, plus(half), b), down).wait_send()
        return carry

    lax.fori_loop(0, half, finish, 0)

    def finish_cross(k, carry):
        o = plus(k)
        for which in range(2):
            x_copy(o, which).wait_send()
            p_copy(o, which).wait_send()
        return carry

    lax.fori_loop(1, nz, finish_cross, 0)


def gathered_projection(states, weights, cosine, sine):
    tokens = states.shape[0]
    pieces, rows, width = weights.shape
    nz = lax.axis_size("dp")
    out = jax.ShapeDtypeStruct((tokens, width), jnp.bfloat16)
    dma = pltpu.SemaphoreType.DMA
    return pl.pallas_call(
        gather_kernel,
        out_shape=(out, jax.ShapeDtypeStruct((2, tokens, width), jnp.bfloat16), jax.ShapeDtypeStruct((nz, rows, width), jnp.bfloat16)),
        in_specs=[pl.BlockSpec(memory_space=VMEM)] * 4,
        out_specs=[pl.BlockSpec(memory_space=VMEM)] * 3,
        scratch_shapes=[
            VMEM((nz, pieces, rows, width), jnp.bfloat16),
            VMEM((3, tokens, width), jnp.float32),
            dma(()),
            dma((pieces, nz)), dma((pieces, nz)),
            dma((2, nz)), dma((2, nz)), dma((2, nz)), dma((2, nz)),
        ],
        compiler_params=pltpu.CompilerParams(collective_id=0, has_side_effects=True),
    )(states, weights, cosine, sine)


def attend_kernel(shard_ref, len_ref, x_ref, q_ref, kv_ref, o_ref, layer_ref, shelf_ref,
                  side, ctx, w3, layer_buf, send_pool, pools, route, shelves,
                  hs, hr, cs, cr, ws, wr, ps, pr, ls, ss, sr, rs, rr):
    ns = lax.axis_size("seq")
    ny = lax.axis_size("index")
    s = lax.axis_index("seq")
    y = lax.axis_index("index")
    core = lax.rem(s, 2)
    partner = s + 1 - 2 * core
    tokens, width = q_ref.shape
    pairs = width // 128
    quarter = layer_ref.shape[1]

    def remote(src, dst, send, recv, device):
        return pltpu.make_async_remote_copy(src_ref=src, dst_ref=dst, send_sem=send, recv_sem=recv,
                                            device_id=device, device_id_type=MESH)

    barrier = pltpu.get_barrier_semaphore()
    for k in range(1, ns):
        pl.semaphore_signal(barrier, inc=1, device_id={"seq": lax.rem(s + k, ns)}, device_id_type=MESH)
    for k in range(1, ny):
        pl.semaphore_signal(barrier, inc=1, device_id={"index": lax.rem(y + k, ny)}, device_id_type=MESH)
    pl.semaphore_wait(barrier, ns + ny - 2)

    after = {"seq": lax.rem(s + 1, ns)}
    before = {"seq": lax.rem(s + ns - 1, ns)}

    def halo_copy(which, pair):
        ref = kv_ref.at[:, :, pl.ds(pair * 128, 128)]
        return remote(ref, side.at[which, pair], hs.at[which, pair], hr.at[which, pair], (after, before)[which])

    for pair in range(pairs):
        for which in range(2):
            halo_copy(which, pair).start()

    owned = o_ref.shape[0] // ny

    def w_copy(k):
        t = lax.rem(y + k, ny)
        src = o_ref.at[pl.ds(t * owned + 2 * core, 2)]
        return remote(src, w3.at[y, pl.ds(2 * core, 2)], ws.at[k], wr.at[y], {"index": t})

    def w_wait(k):
        f = lax.rem(y + k, ny)
        ref = w3.at[f, pl.ds(2 * core, 2)]
        remote(ref, ref, ws.at[k], wr.at[f], {"index": f}).wait_recv()

    def mate_copy(k):
        f = lax.rem(y + k, ny)
        ref = w3.at[f, pl.ds(2 * core, 2)]
        return remote(ref, ref, ps.at[f], pr.at[f], {"seq": partner})

    def mate_wait(k):
        f = lax.rem(y + k, ny)
        ref = w3.at[f, pl.ds(2 - 2 * core, 2)]
        remote(ref, ref, ps.at[f], pr.at[f], {"seq": partner}).wait_recv()

    for k in (1, 3, 2):
        w_copy(k).start()
    own = pltpu.make_async_copy(o_ref.at[pl.ds(y * owned, owned)], w3.at[y], ls)
    own.start()

    row = lax.broadcasted_iota(jnp.int32, (tokens, tokens), 0)
    col = lax.broadcasted_iota(jnp.int32, (tokens, tokens), 1)
    see_before = jnp.logical_and(col >= row, s > 0)
    see_after = jnp.logical_and(col <= row, s < ns - 1)
    lane = lax.broadcasted_iota(jnp.int32, (tokens, 128), 1)

    def ctx_copy(pair, k):
        t = lax.rem(y + k, ny)
        ref = ctx.at[y, pair]
        return remote(ref, ref, cs.at[pair, k], cr.at[pair, y], {"index": t})

    def ctx_wait(pair, k):
        f = lax.rem(y + k, ny)
        ref = ctx.at[f, pair]
        remote(ref, ref, cs.at[pair, k], cr.at[pair, f], {"index": f}).wait_recv()

    def scores(query, key):
        return lax.dot_general(query, key, (((1,), (1,)), ((), ())), preferred_element_type=jnp.float32)

    for pair in range(pairs):
        cols = pl.ds(pair * 128, 128)
        query = q_ref[:, cols]
        for which in range(2):
            halo_copy(which, pair).wait_recv()
        results = []
        for head in range(2):
            inside = (lane < HD) if head == 0 else (lane >= HD)
            chosen = jnp.where(inside, query, jnp.zeros_like(query))
            low = jnp.where(see_before, scores(chosen, side[0, pair, 0]), -1e30)
            mid = scores(chosen, kv_ref[0, :, cols])
            high = jnp.where(see_after, scores(chosen, side[1, pair, 0]), -1e30)
            top = jnp.max(jnp.maximum(jnp.maximum(low, mid), high), axis=1, keepdims=True)
            low, mid, high = jnp.exp(low - top), jnp.exp(mid - top), jnp.exp(high - top)
            total = jnp.sum(low + mid + high, axis=1, keepdims=True)
            value = jnp.dot(low.astype(jnp.bfloat16), side[0, pair, 1], preferred_element_type=jnp.float32)
            value += jnp.dot(mid.astype(jnp.bfloat16), kv_ref[1, :, cols], preferred_element_type=jnp.float32)
            value += jnp.dot(high.astype(jnp.bfloat16), side[1, pair, 1], preferred_element_type=jnp.float32)
            results.append(value / total)
        ctx[y, pair] = jnp.where(lane < HD, results[0], results[1]).astype(jnp.bfloat16)
        for k in (1, 3, 2):
            ctx_copy(pair, k).start()
        w_wait((1, 3, 2)[pair])
        mate_copy((1, 3, 2)[pair]).start()

    def project(k):
        f = lax.rem(y + k, ny)
        context = jnp.concatenate([ctx[f, pair] for pair in range(pairs)], axis=1)
        return jnp.concatenate([scores(context, w3[f, part]) for part in range(owned)], axis=1)

    own.wait()
    summed = x_ref[:, pl.ds(pl.multiple_of(y * quarter, 128), quarter)].astype(jnp.float32) + project(0)
    for k in (1, 3, 2):
        mate_wait(k)
        for pair in range(pairs):
            ctx_wait(pair, k)
        summed += project(k)
    layer = summed.astype(jnp.bfloat16)
    layer_ref[...] = layer

    count = len_ref.shape[1]
    per_block = count // ns
    slots = ns * 8
    slot = lax.broadcasted_iota(jnp.int32, (slots, count), 0)
    stretch = lax.rem(slot, 8) * ns + slot // 8
    which_stretch = lax.broadcasted_iota(jnp.int32, (slots, count), 1)
    lengths = jnp.broadcast_to(len_ref[...], (slots, count))
    ends = jnp.sum(jnp.where(which_stretch <= stretch, lengths, 0), axis=1, keepdims=True)
    starts = jnp.sum(jnp.where(which_stretch < stretch, lengths, 0), axis=1, keepdims=True)
    position = lax.broadcasted_iota(jnp.int32, (slots, tokens), 1) + s * tokens
    real = lax.rem(lax.broadcasted_iota(jnp.int32, (slots, tokens), 0), 8) < per_block
    inside = jnp.logical_and(jnp.logical_and(position >= starts, position < ends), real)
    member = jnp.where(inside, 1.0, 0.0).astype(jnp.bfloat16)
    partial = jnp.dot(member, layer, preferred_element_type=jnp.float32)
    send_pool[...] = partial.reshape(ns, 8, quarter)

    def pool_copy(k):
        t = lax.rem(s + k, ns)
        return remote(send_pool.at[t], pools.at[s], ss.at[k], sr.at[s], {"seq": t})

    def pool_wait(k):
        f = lax.rem(s + k, ns)
        remote(send_pool.at[f], pools.at[f], ss.at[k], sr.at[f], {"seq": f}).wait_recv()

    for k in range(1, ns):
        pool_copy(k).start()
    pooled = send_pool[s]
    for k in range(1, ns):
        pool_wait(k)
    for k in range(1, ns):
        pooled += pools[lax.rem(s + k, ns)]

    ids = [shard_ref[i] for i in range(per_block)]
    line = lax.broadcasted_iota(jnp.int32, (8, quarter), 0)
    places = []
    for i in range(per_block):
        rank = jnp.int32(0)
        for j in range(i):
            rank += jnp.where(ids[j] == ids[i], 1, 0)
        places.append(ids[i] * (per_block // 2) + rank)
    rows = [jnp.broadcast_to(pooled[i:i + 1], (8, quarter)) for i in range(per_block)]
    for r in range(ny):
        held = jnp.zeros((8, quarter), jnp.float32)
        for i in range(per_block):
            held += jnp.where(line == places[i] - r * (per_block // 2), rows[i], 0.0)
        route[r] = held

    def route_copy(k):
        t = lax.rem(y + k, ny)
        return remote(route.at[t], shelves.at[y], rs.at[k], rr.at[y], {"index": t})

    def route_wait(k):
        f = lax.rem(y + k, ny)
        remote(route.at[f], shelves.at[f], rs.at[k], rr.at[f], {"index": f}).wait_recv()

    for k in range(1, ny):
        route_copy(k).start()
    shelves[y] = route[y]
    for k in range(1, ny):
        route_wait(k)
    found = jnp.concatenate([shelves[f, 0:per_block // 2] for f in range(ny)], axis=1)
    mean = jnp.sum(found * found, axis=1, keepdims=True) / (quarter * ny)
    shelf_ref[...] = found * lax.rsqrt(mean + 1e-6)

    for pair in range(pairs):
        for which in range(2):
            halo_copy(which, pair).wait_send()
        for k in range(1, ny):
            ctx_copy(pair, k).wait_send()
    for k in range(1, ny):
        w_copy(k).wait_send()
        mate_copy(k).wait_send()
        route_copy(k).wait_send()
    for k in range(1, ns):
        pool_copy(k).wait_send()


def attended(shards, lengths, states, queries, pair_kv, out_rows):
    tokens, width = queries.shape
    ny = lax.axis_size("index")
    ns = lax.axis_size("seq")
    nz, rows, _ = out_rows.shape
    pairs = width // 128
    quarter = nz * rows // ny
    slots = shards.shape[0] // 2
    dma = pltpu.SemaphoreType.DMA
    return pl.pallas_call(
        attend_kernel,
        out_shape=(jax.ShapeDtypeStruct((tokens, quarter), jnp.bfloat16),
                   jax.ShapeDtypeStruct((slots, quarter * ny), jnp.float32)),
        in_specs=[pl.BlockSpec(memory_space=pltpu.SMEM)] + [pl.BlockSpec(memory_space=VMEM)] * 5,
        out_specs=[pl.BlockSpec(memory_space=VMEM)] * 2,
        scratch_shapes=[
            VMEM((2, pairs, 2, tokens, 128), jnp.bfloat16),
            VMEM((ny, pairs, tokens, 128), jnp.bfloat16),
            VMEM((ny, nz // ny, rows, width), jnp.bfloat16),
            VMEM((8, 128), jnp.float32),
            VMEM((ns, 8, quarter), jnp.float32), VMEM((ns, 8, quarter), jnp.float32),
            VMEM((ny, 8, quarter), jnp.float32), VMEM((ny, 8, quarter), jnp.float32),
            dma((2, pairs)), dma((2, pairs)), dma((pairs, ny)), dma((pairs, ny)),
            dma((ny,)), dma((ny,)), dma((ny,)), dma((ny,)), dma(()),
            dma((ns,)), dma((ns,)), dma((ny,)), dma((ny,)),
        ],
        compiler_params=pltpu.CompilerParams(collective_id=1, has_side_effects=True),
    )(shards, lengths, states, queries, pair_kv, out_rows)


def body(hidden, proj_weight, stretch_lengths, shard_of):
    states = hidden[0]
    tokens_here = states.shape[0]
    positions = lax.axis_index("seq") * tokens_here + jnp.arange(tokens_here, dtype=jnp.int32)
    cosine, sine = rope_tables(positions, 128)
    queries, pair_kv, out_rows = gathered_projection(states, proj_weight, cosine, sine)
    layer, shelf = attended(shard_of[0, :, 0], stretch_lengths, states, queries, pair_kv, out_rows)
    return (layer[None], shelf[None, None, None])


def solution(mesh):
    in_specs = (P("dp", "seq", None), P(None, "dp", "index"), P("dp", None), P("dp", "seq", None))
    out_specs = (P("dp", "seq", "index"), P("dp", "seq", "index", None, None))
    return jax.shard_map(body, mesh=mesh, in_specs=in_specs, out_specs=out_specs, check_vma=False)
```

```python
import jax
import jax.numpy as jnp
from jax import lax
from jax.experimental import pallas as pl
from jax.experimental.pallas import tpu as pltpu
from jax.sharding import PartitionSpec as P

HD = 64
MESH = pl.DeviceIdType.MESH
VMEM = pltpu.VMEM


def layer_kernel(shard_ref, len_ref, x_hbm, w_hbm, layer_ref, shelf_ref,
                 x_ref, w_all, w3_ring, w3, acc, queries, pair_kv, side, ctx, send_pool, pools, route, shelves,
                 local, zs, zr, xs, xr, ps, pr, ys, yr, yl, ws, wr, ms, mr,
                 hs, hr, cs, cr, fs, fr, ss, sr, rs, rr):
    nz = lax.axis_size("dp")
    ns = lax.axis_size("seq")
    ny = lax.axis_size("index")
    z = lax.axis_index("dp")
    s = lax.axis_index("seq")
    y = lax.axis_index("index")
    pieces, rows, width = w_hbm.shape
    tokens = x_ref.shape[0]
    pairs = width // 128
    quarter = layer_ref.shape[1]
    owned = nz // ny
    core = lax.rem(s, 2)
    par = lax.rem(s // 2, 2)
    mate = {"seq": s + 1 - 2 * core}
    right = {"seq": lax.rem(s + 2, ns)}
    left = {"seq": lax.rem(s + ns - 2, ns)}
    after = {"seq": lax.rem(s + 1, ns)}
    before = {"seq": lax.rem(s + ns - 1, ns)}

    def remote(src, dst, send, recv, device):
        return pltpu.make_async_remote_copy(src_ref=src, dst_ref=dst, send_sem=send, recv_sem=recv,
                                            device_id=device, device_id_type=MESH)

    def shifted(d):
        return lax.rem(z + nz + d, nz)

    x_load = pltpu.make_async_copy(x_hbm, x_ref, local.at[0])
    x_load.start()
    own_load = pltpu.make_async_copy(w_hbm.at[pl.ds(0, 3)], w_all.at[z], local.at[1])
    own_load.start()

    barrier = pltpu.get_barrier_semaphore()
    for d in (1, -1):
        pl.semaphore_signal(barrier, inc=1, device_id={"dp": shifted(d)}, device_id_type=MESH)
    for k in range(1, ns):
        pl.semaphore_signal(barrier, inc=1, device_id={"seq": lax.rem(s + k, ns)}, device_id_type=MESH)
    for k in range(1, ny):
        pl.semaphore_signal(barrier, inc=1, device_id={"index": lax.rem(y + k, ny)}, device_id_type=MESH)
    pl.semaphore_wait(barrier, ns + ny)

    part = rows // 4
    sub = part // 2
    mine = pl.multiple_of(rows // 2 * par + part * core, 16)
    other = pl.multiple_of(rows // 2 * (1 - par) + part * core, 16)
    mate_mine = pl.multiple_of(rows // 2 * par + part * (1 - core), 16)
    mate_other = pl.multiple_of(rows // 2 * (1 - par) + part * (1 - core), 16)

    far = nz // 2
    edges = {}
    for d in range(far):
        for sign in ((1, -1) if d < far - 1 else (1,)):
            edges[sign * d, sign * (d + 1)] = len(edges)

    def z_ref(g, o):
        return w3_ring.at[o] if g == 3 else w_all.at[o, g, pl.ds(mine, part)]

    def z_copy(g, here, there):
        o = shifted(-here)
        dst = z_ref(g, o)
        src = w_hbm.at[g, pl.ds(mine, part)] if here == 0 else dst
        return remote(src, dst, zs.at[g, edges[here, there]], zr.at[g, o], {"dp": shifted(there - here)})

    def z_wait(g, d):
        o = shifted(-d)
        remote(z_ref(g, o), z_ref(g, o), zs.at[g, 0], zr.at[g, o], {"dp": shifted(1)}).wait_recv()

    def forward(g, d):
        for here, there in edges:
            if here == d:
                z_copy(g, here, there).start()

    def x_copy(o, which):
        ref = w_all.at[o, :, pl.ds(mine + which * sub, sub)]
        return remote(ref, ref, xs.at[which, o], xr.at[which, o], (right, left)[which])

    def x_wait(o, which):
        ref = w_all.at[o, :, pl.ds(other + which * sub, sub)]
        remote(ref, ref, xs.at[which, o], xr.at[which, o], right).wait_recv()

    def p_copy(o, which):
        ref = w_all.at[o, :, pl.ds((mine, other)[which], part)]
        return remote(ref, ref, ps.at[which, o], pr.at[which, o], mate)

    def p_wait(o, which):
        ref = w_all.at[o, :, pl.ds((mate_mine, mate_other)[which], part)]
        remote(ref, ref, ps.at[which, o], pr.at[which, o], mate).wait_recv()

    def y_local(d):
        o = shifted(-d)
        src = w_hbm.at[3, pl.ds(mine, part)] if d == 0 else w3_ring.at[o]
        j = lax.rem(o, owned)
        return pltpu.make_async_copy(src, w3.at[y, j, pl.ds(mine, part)], yl.at[j])

    def y_copy(d):
        o = shifted(-d)
        src = w_hbm.at[3, pl.ds(mine, part)] if d == 0 else w3_ring.at[o]
        j = lax.rem(o, owned)
        return remote(src, w3.at[y, j, pl.ds(mine, part)], ys.at[o], yr.at[y, j], {"index": o // owned})

    def y_start(d):
        stays = shifted(-d) // owned == y

        @pl.when(stays)
        def _():
            y_local(d).start()

        @pl.when(jnp.logical_not(stays))
        def _():
            y_copy(d).start()

    def y_finish(d):
        @pl.when(shifted(-d) // owned != y)
        def _():
            y_copy(d).wait_send()

    def w_copy(j, which):
        ref = w3.at[:, j, pl.ds(mine + which * sub, sub)]
        return remote(ref, ref, ws.at[which, j], wr.at[which, j], (right, left)[which])

    def w_wait(j, which):
        ref = w3.at[:, j, pl.ds(other + which * sub, sub)]
        remote(ref, ref, ws.at[which, j], wr.at[which, j], right).wait_recv()

    def m_copy(j, which):
        ref = w3.at[:, j, pl.ds((mine, other)[which], part)]
        return remote(ref, ref, ms.at[which, j], mr.at[which, j], mate)

    def m_wait(j, which):
        ref = w3.at[:, j, pl.ds((mate_mine, mate_other)[which], part)]
        remote(ref, ref, ms.at[which, j], mr.at[which, j], mate).wait_recv()

    def w_arrive(d):
        o = shifted(-d)
        j = lax.rem(o, owned)

        @pl.when(o // owned == y)
        def _():
            y_local(d).wait()
            for k in range(1, ny):
                f = lax.rem(y + k, ny)
                ref = w3.at[f, j, pl.ds(mine, part)]
                remote(ref, ref, ys.at[0], yr.at[f, j], {"index": f}).wait_recv()
            for which in range(2):
                w_copy(j, which).start()
            m_copy(j, 0).start()

    def w_cross(d):
        o = shifted(-d)
        j = lax.rem(o, owned)

        @pl.when(o // owned == y)
        def _():
            for which in range(2):
                w_wait(j, which)
            m_copy(j, 1).start()

    for g in range(pieces):
        forward(g, 0)
    y_start(0)

    half = HD // 2
    lane = lax.broadcasted_iota(jnp.int32, (tokens, 128), 1)
    lower = lax.rem(lane, HD) < half
    freqs = jnp.exp(lax.rem(lane, half).astype(jnp.float32) * (-2.0 / HD * 9.210340371976184))
    angles = (lax.broadcasted_iota(jnp.int32, (tokens, 128), 0) + s * tokens).astype(jnp.float32) * freqs
    cosine = jnp.cos(angles)
    sine = jnp.sin(angles)
    sine = jnp.where(lower, -sine, sine)

    acc[...] = jnp.zeros_like(acc)
    x_load.wait()
    own_load.wait()

    def arrive(ds):
        for d in ds:
            for g in range(3):
                z_wait(g, d)
                forward(g, d)
            for which in range(2):
                x_copy(shifted(-d), which).start()
            p_copy(shifted(-d), 0).start()
        for d in ds:
            z_wait(3, d)
            forward(3, d)
            y_start(d)

    def cross(ds):
        for d in ds:
            for which in range(2):
                x_wait(shifted(-d), which)
            p_copy(shifted(-d), 1).start()

    def settle(ds):
        for d in ds:
            for which in range(2):
                p_wait(shifted(-d), which)
        a, b = (shifted(-d) for d in (ds if len(ds) == 2 else (0, ds[0])))
        lhs = jnp.concatenate([x_ref[:, pl.ds(pl.multiple_of(o * rows, 128), rows)] for o in (a, b)], axis=1)
        for j in range(3):
            rhs = jnp.concatenate([w_all[a, j], w_all[b, j]], axis=0)
            acc[j] += jnp.dot(lhs, rhs, preferred_element_type=jnp.float32)

    order = [(d, -d) for d in range(1, far)] + [(far,)]
    for i in range(len(order) + 2):
        if i < len(order):
            arrive(order[i])
        if 1 <= i <= len(order):
            cross(order[i - 1])
            for d in order[i - 1] + ((0,) if i == 1 else ()):
                w_arrive(d)
        if i >= 2:
            settle(order[i - 2])
            for d in order[i - 2] + ((0,) if i == 2 else ()):
                w_cross(d)

    for j in (1, 0):
        for pair in range(pairs):
            cols = slice(pair * 128, pair * 128 + 128)
            value = acc[j, :, cols]
            swapped = jnp.where(lower, pltpu.roll(value, 128 - half, 1), pltpu.roll(value, half, 1))
            turned = value * cosine + swapped * sine
            if j == 0:
                queries[pair] = (turned * HD ** -0.5).astype(jnp.bfloat16)
            else:
                pair_kv[pair, 0] = turned.astype(jnp.bfloat16)
                pair_kv[pair, 1] = acc[2, :, cols].astype(jnp.bfloat16)
                for which in range(2):
                    remote(pair_kv.at[pair], side.at[which, pair], hs.at[which, pair], hr.at[which, pair],
                           (after, before)[which]).start()

    def halo(which, pair):
        return remote(pair_kv.at[pair], side.at[which, pair], hs.at[which, pair], hr.at[which, pair],
                      (after, before)[which])

    row = lax.broadcasted_iota(jnp.int32, (tokens, tokens), 0)
    col = lax.broadcasted_iota(jnp.int32, (tokens, tokens), 1)
    see_before = jnp.logical_and(col >= row, s > 0)
    see_after = jnp.logical_and(col <= row, s < ns - 1)

    def beside(k):
        return {"index": lax.rem(y + k, ny)}

    def c_copy(pair, k):
        ref = ctx.at[y, pair]
        return remote(ref, ref, cs.at[pair, k], cr.at[pair, y], beside(k))

    def c_wait(pair, k):
        f = lax.rem(y + k, ny)
        ref = ctx.at[f, pair]
        remote(ref, ref, cs.at[pair, k], cr.at[pair, f], beside(k)).wait_recv()

    def f_copy(pair, k):
        f = lax.rem(y + k, ny)
        ref = ctx.at[f, pair, pl.ds(0 if k == 3 else tokens // 2, tokens // 2)]
        return remote(ref, ref, fs.at[pair, k // 2], fr.at[pair, k // 2], beside(ny - k))

    def f_wait(pair, k):
        f = lax.rem(y + 2, ny)
        ref = ctx.at[f, pair, pl.ds(0 if k == 3 else tokens // 2, tokens // 2)]
        remote(ref, ref, fs.at[pair, k // 2], fr.at[pair, k // 2], beside(k)).wait_recv()

    def relay(pair):
        for k in (1, 3):
            c_wait(pair, k)
            f_copy(pair, k).start()

    def scores(query, key):
        return lax.dot_general(query, key, (((1,), (1,)), ((), ())), preferred_element_type=jnp.float32)

    for pair in range(pairs):
        query = queries[pair]
        for which in range(2):
            halo(which, pair).wait_recv()
        results = []
        for head in range(2):
            inside = (lane < HD) if head == 0 else (lane >= HD)
            chosen = jnp.where(inside, query, jnp.zeros_like(query))
            low = jnp.where(see_before, scores(chosen, side[0, pair, 0]), -1e30)
            mid = scores(chosen, pair_kv[pair, 0])
            high = jnp.where(see_after, scores(chosen, side[1, pair, 0]), -1e30)
            top = jnp.max(jnp.maximum(jnp.maximum(low, mid), high), axis=1, keepdims=True)
            low, mid, high = jnp.exp(low - top), jnp.exp(mid - top), jnp.exp(high - top)
            total = jnp.sum(low + mid + high, axis=1, keepdims=True)
            value = jnp.dot(low.astype(jnp.bfloat16), side[0, pair, 1], preferred_element_type=jnp.float32)
            value += jnp.dot(mid.astype(jnp.bfloat16), pair_kv[pair, 1], preferred_element_type=jnp.float32)
            value += jnp.dot(high.astype(jnp.bfloat16), side[1, pair, 1], preferred_element_type=jnp.float32)
            results.append(value / total)
        ctx[y, pair] = jnp.where(lane < HD, results[0], results[1]).astype(jnp.bfloat16)
        for k in (1, 3):
            c_copy(pair, k).start()
        if pair > 0:
            relay(pair - 1)

    def project(k):
        f = lax.rem(y + k, ny)
        context = jnp.concatenate([ctx[f, pair] for pair in range(pairs)], axis=1)
        return jnp.concatenate([scores(context, w3[f, j]) for j in range(owned)], axis=1)

    for j in range(owned):
        for which in range(2):
            m_wait(j, which)
    summed = x_ref[:, pl.ds(pl.multiple_of(y * quarter, 128), quarter)].astype(jnp.float32) + project(0)
    relay(pairs - 1)
    summed += project(1)
    summed += project(3)
    for pair in range(pairs):
        for k in (1, 3):
            f_wait(pair, k)
    summed += project(2)
    layer = summed.astype(jnp.bfloat16)
    layer_ref[...] = layer

    count = len_ref.shape[1]
    per_block = count // ns
    slots = ns * 8
    slot = lax.broadcasted_iota(jnp.int32, (slots, count), 0)
    stretch = lax.rem(slot, 8) * ns + slot // 8
    which_stretch = lax.broadcasted_iota(jnp.int32, (slots, count), 1)
    lengths = jnp.broadcast_to(len_ref[...], (slots, count))
    ends = jnp.sum(jnp.where(which_stretch <= stretch, lengths, 0), axis=1, keepdims=True)
    starts = jnp.sum(jnp.where(which_stretch < stretch, lengths, 0), axis=1, keepdims=True)
    position = lax.broadcasted_iota(jnp.int32, (slots, tokens), 1) + s * tokens
    real = lax.rem(lax.broadcasted_iota(jnp.int32, (slots, tokens), 0), 8) < per_block
    inside = jnp.logical_and(jnp.logical_and(position >= starts, position < ends), real)
    member = jnp.where(inside, 1.0, 0.0).astype(jnp.bfloat16)
    partial = jnp.dot(member, layer, preferred_element_type=jnp.float32)
    send_pool[...] = partial.reshape(ns, 8, quarter)

    def pool_copy(k):
        t = lax.rem(s + k, ns)
        return remote(send_pool.at[t], pools.at[s], ss.at[k], sr.at[s], {"seq": t})

    def pool_wait(k):
        f = lax.rem(s + k, ns)
        remote(send_pool.at[f], pools.at[f], ss.at[k], sr.at[f], {"seq": f}).wait_recv()

    for k in range(1, ns):
        pool_copy(k).start()
    pooled = send_pool[s]
    for k in range(1, ns):
        pool_wait(k)
    for k in range(1, ns):
        pooled += pools[lax.rem(s + k, ns)]

    ids = [shard_ref[i] for i in range(per_block)]
    line = lax.broadcasted_iota(jnp.int32, (8, quarter), 0)
    places = []
    for i in range(per_block):
        rank = jnp.int32(0)
        for j in range(i):
            rank += jnp.where(ids[j] == ids[i], 1, 0)
        places.append(ids[i] * (per_block // 2) + rank)
    lines = [jnp.broadcast_to(pooled[i:i + 1], (8, quarter)) for i in range(per_block)]
    for r in range(ny):
        held = jnp.zeros((8, quarter), jnp.float32)
        for i in range(per_block):
            held += jnp.where(line == places[i] - r * (per_block // 2), lines[i], 0.0)
        route[r] = held

    def route_copy(k):
        t = lax.rem(y + k, ny)
        return remote(route.at[t], shelves.at[y], rs.at[k], rr.at[y], {"index": t})

    def route_wait(k):
        f = lax.rem(y + k, ny)
        remote(route.at[f], shelves.at[f], rs.at[k], rr.at[f], {"index": f}).wait_recv()

    for k in range(1, ny):
        route_copy(k).start()
    shelves[y] = route[y]

    for g in range(pieces):
        for here, there in edges:
            z_copy(g, here, there).wait_send()
    for d in (0,) + tuple(d for ds in order for d in ds):
        y_finish(d)
        if d:
            for which in range(2):
                x_copy(shifted(-d), which).wait_send()
                p_copy(shifted(-d), which).wait_send()
    for j in range(owned):
        for which in range(2):
            w_copy(j, which).wait_send()
            m_copy(j, which).wait_send()
    for pair in range(pairs):
        for which in range(2):
            halo(which, pair).wait_send()
        for k in (1, 3):
            c_copy(pair, k).wait_send()
            f_copy(pair, k).wait_send()
    for k in range(1, ns):
        pool_copy(k).wait_send()

    for k in range(1, ny):
        route_wait(k)
    found = jnp.concatenate([shelves[f, 0:per_block // 2] for f in range(ny)], axis=1)
    mean = jnp.sum(found * found, axis=1, keepdims=True) / (quarter * ny)
    shelf_ref[...] = found * lax.rsqrt(mean + 1e-6)
    for k in range(1, ny):
        route_copy(k).wait_send()


def body(hidden, proj_weight, stretch_lengths, shard_of):
    states = hidden[0]
    tokens, depth = states.shape
    pieces, rows, width = proj_weight.shape
    nz, ns, ny = (lax.axis_size(a) for a in ("dp", "seq", "index"))
    pairs = width // 128
    quarter = depth // ny
    slots = shard_of.shape[1] // 2
    dma = pltpu.SemaphoreType.DMA
    bf16, f32 = jnp.bfloat16, jnp.float32
    any_space = pl.BlockSpec(memory_space=pl.ANY)
    vmem_space = pl.BlockSpec(memory_space=VMEM)
    layer, shelf = pl.pallas_call(
        layer_kernel,
        out_shape=(jax.ShapeDtypeStruct((tokens, quarter), bf16), jax.ShapeDtypeStruct((slots, depth), f32)),
        in_specs=[pl.BlockSpec(memory_space=pltpu.SMEM), vmem_space, any_space, any_space],
        out_specs=[vmem_space] * 2,
        scratch_shapes=[
            VMEM((tokens, depth), bf16),
            VMEM((nz, 3, rows, width), bf16),
            VMEM((nz, rows // 4, width), bf16),
            VMEM((ny, nz // ny, rows, width), bf16),
            VMEM((3, tokens, width), f32),
            VMEM((pairs, tokens, 128), bf16),
            VMEM((pairs, 2, tokens, 128), bf16),
            VMEM((2, pairs, 2, tokens, 128), bf16),
            VMEM((ny, pairs, tokens, 128), bf16),
            VMEM((ns, 8, quarter), f32), VMEM((ns, 8, quarter), f32),
            VMEM((ny, 8, quarter), f32), VMEM((ny, 8, quarter), f32),
            dma((2,)),
            dma((pieces, nz - 1)), dma((pieces, nz)),
            dma((2, nz)), dma((2, nz)), dma((2, nz)), dma((2, nz)),
            dma((nz,)), dma((ny, nz // ny)), dma((nz // ny,)),
            dma((2, nz // ny)), dma((2, nz // ny)), dma((2, nz // ny)), dma((2, nz // ny)),
            dma((2, pairs)), dma((2, pairs)), dma((pairs, ny)), dma((pairs, ny)), dma((pairs, 2)), dma((pairs, 2)),
            dma((ns,)), dma((ns,)), dma((ny,)), dma((ny,)),
        ],
        compiler_params=pltpu.CompilerParams(collective_id=0, has_side_effects=True),
    )(shard_of[0, :, 0], stretch_lengths, states, proj_weight)
    return (layer[None], shelf[None, None, None])


def solution(mesh):
    in_specs = (P("dp", "seq", None), P(None, "dp", "index"), P("dp", None), P("dp", "seq", None))
    out_specs = (P("dp", "seq", "index"), P("dp", "seq", "index", None, None))
    return jax.shard_map(body, mesh=mesh, in_specs=in_specs, out_specs=out_specs, check_vma=False)
```

```python
import jax
import jax.numpy as jnp
from jax import lax
from jax.experimental import pallas as pl
from jax.experimental.pallas import tpu as pltpu
from jax.sharding import PartitionSpec as P

HD = 64
MESH = pl.DeviceIdType.MESH
VMEM = pltpu.VMEM


def layer_kernel(shard_ref, len_ref, x_hbm, w_hbm, layer_ref, shelf_ref,
                 x_ref, near_x, w_all, w3_ring, w3, acc, near_acc, tables, queries, pair_kv, side, ctx,
                 id_send, id_all, member, send_rows, got,
                 local, zs, zr, xs, xr, ps, pr, ys, yr, yl, ws, wr, ms, mr,
                 ns_, nr, hs, hr, cs, cr, fs, fr, is_, ir, gs, gr):
    nz = lax.axis_size("dp")
    ns = lax.axis_size("seq")
    ny = lax.axis_size("index")
    z = lax.axis_index("dp")
    s = lax.axis_index("seq")
    y = lax.axis_index("index")
    pieces, rows, width = w_hbm.shape
    tokens = x_ref.shape[0]
    pairs = width // 128
    quarter = layer_ref.shape[1]
    owned = nz // ny
    core = lax.rem(s, 2)
    par = lax.rem(s // 2, 2)
    mate = {"seq": s + 1 - 2 * core}
    right = {"seq": lax.rem(s + 2, ns)}
    left = {"seq": lax.rem(s + ns - 2, ns)}
    near = s + 2 * core - 1
    neighbour = {"seq": lax.rem(near + ns, ns)}
    me = s * ny + y
    count = len_ref.shape[1]
    per_block = count // ns
    capacity = per_block // 2

    def remote(src, dst, send, recv, device):
        return pltpu.make_async_remote_copy(src_ref=src, dst_ref=dst, send_sem=send, recv_sem=recv,
                                            device_id=device, device_id_type=MESH)

    def shifted(d):
        return lax.rem(z + nz + d, nz)

    x_load = pltpu.make_async_copy(x_hbm, x_ref, local.at[0])
    x_load.start()
    own_load = pltpu.make_async_copy(w_hbm.at[pl.ds(0, 3)], w_all.at[z], local.at[1])
    own_load.start()

    barrier = pltpu.get_barrier_semaphore()
    for d in (1, -1):
        pl.semaphore_signal(barrier, inc=1, device_id={"dp": shifted(d)}, device_id_type=MESH)

    def greet(k, carry):
        t = lax.rem(me + k, ns * ny)
        pl.semaphore_signal(barrier, inc=1, device_id={"seq": t // ny, "index": lax.rem(t, ny)}, device_id_type=MESH)
        return carry

    lax.fori_loop(1, ns * ny, greet, 0)
    tile_row = lax.broadcasted_iota(jnp.int32, (8, 128), 0)
    ids = jnp.zeros((8, 128), jnp.int32)
    for i in range(per_block):
        ids = jnp.where(tile_row == i, shard_ref[i], ids)
    id_send[...] = ids
    id_all[s] = ids
    pl.semaphore_wait(barrier, ns * ny + 1)

    part = rows // 4
    sub = part // 2
    mine = pl.multiple_of(rows // 2 * par + part * core, 16)
    other = pl.multiple_of(rows // 2 * (1 - par) + part * core, 16)
    mate_mine = pl.multiple_of(rows // 2 * par + part * (1 - core), 16)
    mate_other = pl.multiple_of(rows // 2 * (1 - par) + part * (1 - core), 16)

    far = nz // 2
    edges = {}
    for d in range(far):
        for sign in ((1, -1) if d < far - 1 else (1,)):
            edges[sign * d, sign * (d + 1)] = len(edges)

    def z_ref(g, o):
        return w3_ring.at[o] if g == 3 else w_all.at[o, g, pl.ds(mine, part)]

    def z_copy(g, here, there):
        o = shifted(-here)
        dst = z_ref(g, o)
        src = w_hbm.at[g, pl.ds(mine, part)] if here == 0 else dst
        return remote(src, dst, zs.at[g, edges[here, there]], zr.at[g, o], {"dp": shifted(there - here)})

    def z_wait(g, d):
        o = shifted(-d)
        remote(z_ref(g, o), z_ref(g, o), zs.at[g, 0], zr.at[g, o], {"dp": shifted(1)}).wait_recv()

    def forward(g, d):
        for here, there in edges:
            if here == d:
                z_copy(g, here, there).start()

    def x_copy(o, which):
        ref = w_all.at[o, :, pl.ds(mine + which * sub, sub)]
        return remote(ref, ref, xs.at[which, o], xr.at[which, o], (right, left)[which])

    def x_wait(o, which):
        ref = w_all.at[o, :, pl.ds(other + which * sub, sub)]
        remote(ref, ref, xs.at[which, o], xr.at[which, o], right).wait_recv()

    def p_copy(o, which):
        ref = w_all.at[o, :, pl.ds((mine, other)[which], part)]
        return remote(ref, ref, ps.at[which, o], pr.at[which, o], mate)

    def p_wait(o, which):
        ref = w_all.at[o, :, pl.ds((mate_mine, mate_other)[which], part)]
        remote(ref, ref, ps.at[which, o], pr.at[which, o], mate).wait_recv()

    def y_local(d):
        o = shifted(-d)
        src = w_hbm.at[3, pl.ds(mine, part)] if d == 0 else w3_ring.at[o]
        j = lax.rem(o, owned)
        return pltpu.make_async_copy(src, w3.at[y, j, pl.ds(mine, part)], yl.at[j])

    def y_copy(d):
        o = shifted(-d)
        src = w_hbm.at[3, pl.ds(mine, part)] if d == 0 else w3_ring.at[o]
        j = lax.rem(o, owned)
        return remote(src, w3.at[y, j, pl.ds(mine, part)], ys.at[o], yr.at[y, j], {"index": o // owned})

    def y_start(d):
        stays = shifted(-d) // owned == y

        @pl.when(stays)
        def _():
            y_local(d).start()

        @pl.when(jnp.logical_not(stays))
        def _():
            y_copy(d).start()

    def y_finish(d):
        @pl.when(shifted(-d) // owned != y)
        def _():
            y_copy(d).wait_send()

    def w_copy(j, which):
        ref = w3.at[:, j, pl.ds(mine + which * sub, sub)]
        return remote(ref, ref, ws.at[which, j], wr.at[which, j], (right, left)[which])

    def w_wait(j, which):
        ref = w3.at[:, j, pl.ds(other + which * sub, sub)]
        remote(ref, ref, ws.at[which, j], wr.at[which, j], right).wait_recv()

    def m_copy(j, which):
        ref = w3.at[:, j, pl.ds((mine, other)[which], part)]
        return remote(ref, ref, ms.at[which, j], mr.at[which, j], mate)

    def m_wait(j, which):
        ref = w3.at[:, j, pl.ds((mate_mine, mate_other)[which], part)]
        remote(ref, ref, ms.at[which, j], mr.at[which, j], mate).wait_recv()

    def w_arrive(d):
        o = shifted(-d)
        j = lax.rem(o, owned)

        @pl.when(o // owned == y)
        def _():
            y_local(d).wait()
            for k in range(1, ny):
                f = lax.rem(y + k, ny)
                ref = w3.at[f, j, pl.ds(mine, part)]
                remote(ref, ref, ys.at[0], yr.at[f, j], {"index": f}).wait_recv()
            for which in range(2):
                w_copy(j, which).start()
            m_copy(j, 0).start()

    def w_cross(d):
        o = shifted(-d)
        j = lax.rem(o, owned)

        @pl.when(o // owned == y)
        def _():
            for which in range(2):
                w_wait(j, which)
            m_copy(j, 1).start()

    def beside(k):
        return {"index": lax.rem(y + k, ny)}

    share = tokens // ny

    def n_rows(k, lower_half=None):
        f = lax.rem(y + k, ny)
        if lower_half is None:
            return near_x.at[pl.ds(pl.multiple_of(f * share, share), share)]
        start = f * share + (0 if lower_half else share // 2)
        return near_x.at[pl.ds(pl.multiple_of(start, share // 2), share // 2)]

    def n_first():
        src = x_hbm.at[pl.ds(pl.multiple_of(y * share, share), share)]
        return remote(src, n_rows(0), ns_.at[0], nr.at[0], neighbour)

    def n_copy(k):
        return remote(n_rows(0), n_rows(0), ns_.at[k], nr.at[4 - k], beside(k))

    def n_wait(k):
        remote(n_rows(k), n_rows(k), ns_.at[k], nr.at[k], beside(k)).wait_recv()

    def n_relay(k):
        ref = n_rows(k, k == 3)
        return remote(ref, ref, ns_.at[3 + k], nr.at[3 + k], beside(ny - k))

    def n_relay_wait(k):
        ref = n_rows(2, k == 3)
        remote(ref, ref, ns_.at[3 + k], nr.at[3 + k], beside(k)).wait_recv()

    def i_copy(k):
        t = lax.rem(s + k, ns)
        return remote(id_send, id_all.at[s], is_.at[k], ir.at[s], {"seq": t})

    for g in range(pieces):
        forward(g, 0)
    y_start(0)
    n_first().start()
    for k in range(1, ns):
        i_copy(k).start()

    half = HD // 2
    lane = lax.broadcasted_iota(jnp.int32, (tokens, 128), 1)
    lower = lax.rem(lane, HD) < half
    freqs = jnp.exp(lax.rem(lane, half).astype(jnp.float32) * (-2.0 / HD * 9.210340371976184))
    token = lax.broadcasted_iota(jnp.int32, (tokens, 128), 0)

    def fill_tables(i, block):
        angles = (token + block * tokens).astype(jnp.float32) * freqs
        tables[2 * i] = jnp.cos(angles)
        sine = jnp.sin(angles)
        tables[2 * i + 1] = jnp.where(lower, -sine, sine)


    def arrive(ds):
        for d in ds:
            for g in range(3):
                z_wait(g, d)
                forward(g, d)
            for which in range(2):
                x_copy(shifted(-d), which).start()
            p_copy(shifted(-d), 0).start()
        for d in ds:
            z_wait(3, d)
            forward(3, d)
            y_start(d)

    def cross(ds):
        for d in ds:
            for which in range(2):
                x_wait(shifted(-d), which)
            p_copy(shifted(-d), 1).start()

    def lhs_of(ref, ds):
        return jnp.concatenate([ref[:, pl.ds(pl.multiple_of(o * rows, 128), rows)] for o in origins(ds)], axis=1)

    def origins(ds):
        return [shifted(-d) for d in (ds if len(ds) == 2 else (0, ds[0]))]

    def rhs_of(j, ds):
        return jnp.concatenate([w_all[o, j] for o in origins(ds)], axis=0)

    def near_multiply(ds, first):
        lhs = lhs_of(near_x, ds)
        for j in (1, 2):
            product = jnp.dot(lhs, rhs_of(j, ds), preferred_element_type=jnp.float32)
            near_acc[j - 1] = product if first else near_acc[j - 1] + product

    def settle(ds, first, both):
        for d in ds:
            for which in range(2):
                p_wait(shifted(-d), which)
        lhs = lhs_of(x_ref, ds)
        product = jnp.dot(lhs, rhs_of(0, ds), preferred_element_type=jnp.float32)
        acc[0] = product if first else acc[0] + product
        if both:
            lhs = jnp.concatenate([lhs, lhs_of(near_x, ds)], axis=0)
        for j in (1, 2):
            product = jnp.dot(lhs, rhs_of(j, ds), preferred_element_type=jnp.float32)
            acc[j] = product[:tokens] if first else acc[j] + product[:tokens]
            if both:
                near_acc[j - 1] += product[tokens:]

    def place_stretches():
        for k in range(1, ns):
            f = lax.rem(s + k, ns)
            remote(id_all.at[f], id_all.at[f], is_.at[k], ir.at[f], {"seq": f}).wait_recv()
        slots = ns * 8
        slot = lax.broadcasted_iota(jnp.int32, (slots, count), 0)
        stretch = lax.rem(slot, 8) * ns + slot // 8
        which_stretch = lax.broadcasted_iota(jnp.int32, (slots, count), 1)
        lengths = jnp.broadcast_to(len_ref[...], (slots, count))
        cube = (ns, 8, 128)

        def wide(picked):
            return jnp.broadcast_to(jnp.sum(jnp.where(picked, lengths, 0), axis=1, keepdims=True), (slots, 128)).reshape(cube)

        ends = wide(which_stretch <= stretch)
        starts = wide(which_stretch < stretch)
        line = lax.broadcasted_iota(jnp.int32, cube, 1)
        shard = id_all[...]

        def spread(value, i):
            return jnp.broadcast_to(value[:, i:i + 1, :], cube)

        rank = jnp.zeros(cube, jnp.int32)
        for i in range(per_block - 1):
            rank += jnp.where(jnp.logical_and(spread(shard, i) == shard, line > i), 1, 0)
        place = shard * capacity + rank
        first = jnp.zeros(cube, jnp.int32)
        last = jnp.zeros(cube, jnp.int32)
        for i in range(per_block):
            here = spread(place, i) == line
            first = jnp.where(here, spread(starts, i), first)
            last = jnp.where(here, spread(ends, i), last)
        first, last = first.reshape(slots, 128), last.reshape(slots, 128)
        for start in range(0, tokens, 128):
            position = lax.broadcasted_iota(jnp.int32, (slots, 128), 1) + (s * tokens + start)
            inside = jnp.logical_and(position >= first, position < last)
            member[:, start:start + 128] = jnp.where(inside, 1.0, 0.0).astype(jnp.bfloat16)

    order = [(d, -d) for d in range(1, far)] + [(far,)]
    turns = len(order) + 2
    for i in range(turns):
        if i < len(order):
            arrive(order[i])
        if 1 <= i <= len(order):
            cross(order[i - 1])
        if i == 1:
            n_first().wait_recv()
            for k in (1, 3):
                n_copy(k).start()
            x_load.wait()
            own_load.wait()
        if i == 2:
            place_stretches()
        if i == 3:
            fill_tables(0, s)
        if i == 4:
            for k in (1, 3):
                n_wait(k)
                n_relay(k).start()
        if i == 5:
            fill_tables(1, near)
        if i == 6:
            for k in (1, 3):
                n_relay_wait(k)
        if i in (6, 7):
            for m in (2 * i - 12, 2 * i - 11):
                near_multiply(order[m], m == 0)
        if i >= 2:
            settle(order[i - 2], i == 2, i >= 6)
        if i >= 4:
            for d in order[i - 4] + ((0,) if i == 4 else ()):
                w_arrive(d)
        if i >= 6:
            for d in order[i - 6] + ((0,) if i == 6 else ()):
                w_cross(d)

    def turned(value, i):
        swapped = jnp.where(lower, pltpu.roll(value, 128 - half, 1), pltpu.roll(value, half, 1))
        return value * tables[2 * i] + swapped * tables[2 * i + 1]

    def h_copy(pair):
        return remote(pair_kv.at[pair], side.at[core, pair], hs.at[pair], hr.at[pair], mate)

    def h_wait(pair):
        ref = side.at[1 - core, pair]
        remote(ref, ref, hs.at[pair], hr.at[pair], mate).wait_recv()

    blocks = [slice(pair * 128, pair * 128 + 128) for pair in range(pairs)]
    for pair, cols in enumerate(blocks):
        pair_kv[pair, 0] = turned(acc[1, :, cols], 0).astype(jnp.bfloat16)
        pair_kv[pair, 1] = acc[2, :, cols].astype(jnp.bfloat16)
        h_copy(pair).start()
    for pair, cols in enumerate(blocks):
        side[core, pair, 0] = turned(near_acc[0, :, cols], 1).astype(jnp.bfloat16)
        side[core, pair, 1] = near_acc[1, :, cols].astype(jnp.bfloat16)
        queries[pair] = (turned(acc[0, :, cols], 0) * HD ** -0.5).astype(jnp.bfloat16)

    for ds in order[turns - 4:]:
        for d in ds:
            w_arrive(d)

    strip = tokens // 2

    def c_rows(f, piece, start=0, size=strip):
        return ctx.at[f, piece // 2, pl.ds(piece % 2 * strip + start, size)]

    def c_copy(piece, k):
        ref = c_rows(y, piece)
        return remote(ref, ref, cs.at[piece, k], cr.at[piece, y], beside(k))

    def c_wait(piece, k):
        f = lax.rem(y + k, ny)
        ref = c_rows(f, piece)
        remote(ref, ref, cs.at[piece, k], cr.at[piece, f], beside(k)).wait_recv()

    def f_copy(piece, k):
        ref = c_rows(lax.rem(y + k, ny), piece, 0 if k == 3 else strip // 2, strip // 2)
        return remote(ref, ref, fs.at[piece, k // 2], fr.at[piece, k // 2], beside(ny - k))

    def f_wait(piece, k):
        ref = c_rows(lax.rem(y + 2, ny), piece, 0 if k == 3 else strip // 2, strip // 2)
        remote(ref, ref, fs.at[piece, k // 2], fr.at[piece, k // 2], beside(k)).wait_recv()

    def relay(piece):
        for k in (1, 3):
            c_wait(piece, k)
            f_copy(piece, k).start()

    def scores(query, key):
        return lax.dot_general(query, key, (((1,), (1,)), ((), ())), preferred_element_type=jnp.float32)

    lag = 4
    narrow = lax.broadcasted_iota(jnp.int32, (strip, 128), 1)
    for pair in range(pairs):
        h_wait(pair)
        for part_of in range(2):
            piece = 2 * pair + part_of
            top_row = part_of * strip
            query = queries[pair, top_row:top_row + strip]
            low_keys = slice(top_row, tokens)
            high_keys = slice(0, top_row + strip)
            low_shape = (strip, tokens - top_row)
            high_shape = (strip, top_row + strip)
            see_low = jnp.logical_and(lax.broadcasted_iota(jnp.int32, low_shape, 1) >= lax.broadcasted_iota(jnp.int32, low_shape, 0), s > 0)
            see_high = jnp.logical_and(
                lax.broadcasted_iota(jnp.int32, high_shape, 1) <= lax.broadcasted_iota(jnp.int32, high_shape, 0) + top_row, s < ns - 1)
            results = []
            for head in range(2):
                inside = (narrow < HD) if head == 0 else (narrow >= HD)
                chosen = jnp.where(inside, query, jnp.zeros_like(query))
                low = jnp.where(see_low, scores(chosen, side[0, pair, 0, low_keys]), -1e30)
                mid = scores(chosen, pair_kv[pair, 0])
                high = jnp.where(see_high, scores(chosen, side[1, pair, 0, high_keys]), -1e30)
                top = jnp.maximum(jnp.max(mid, axis=1, keepdims=True), jnp.maximum(
                    jnp.max(low, axis=1, keepdims=True), jnp.max(high, axis=1, keepdims=True)))
                low, mid, high = jnp.exp(low - top), jnp.exp(mid - top), jnp.exp(high - top)
                total = (jnp.sum(low, axis=1, keepdims=True) + jnp.sum(mid, axis=1, keepdims=True)
                         + jnp.sum(high, axis=1, keepdims=True))
                value = jnp.dot(low.astype(jnp.bfloat16), side[0, pair, 1, low_keys], preferred_element_type=jnp.float32)
                value += jnp.dot(mid.astype(jnp.bfloat16), pair_kv[pair, 1], preferred_element_type=jnp.float32)
                value += jnp.dot(high.astype(jnp.bfloat16), side[1, pair, 1, high_keys], preferred_element_type=jnp.float32)
                results.append(value / total)
            ctx[y, pair, top_row:top_row + strip] = jnp.where(narrow < HD, results[0], results[1]).astype(jnp.bfloat16)
            for k in (1, 3):
                c_copy(piece, k).start()
            if piece >= lag:
                relay(piece - lag)
            if piece == 2:
                for ds in order[turns - 6:]:
                    for d in ds:
                        w_cross(d)

    def project(k):
        f = lax.rem(y + k, ny)
        context = jnp.concatenate([ctx[f, pair] for pair in range(pairs)], axis=1)
        return jnp.concatenate([scores(context, w3[f, j]) for j in range(owned)], axis=1)

    for j in range(owned):
        for which in range(2):
            m_wait(j, which)
    summed = x_ref[:, pl.ds(pl.multiple_of(y * quarter, 128), quarter)].astype(jnp.float32) + project(0)
    for piece in range(2 * pairs - lag, 2 * pairs):
        relay(piece)
    summed += project(1)
    summed += project(3)
    for piece in range(2 * pairs):
        for k in (1, 3):
            f_wait(piece, k)
    summed += project(2)
    layer = summed.astype(jnp.bfloat16)
    layer_ref[...] = layer

    partial = jnp.dot(member[...], layer, preferred_element_type=jnp.float32)
    for t in range(ns * ny):
        send_rows[t] = partial[t * capacity:(t + 1) * capacity]

    def g_copy(k):
        t = lax.rem(me + k, ns * ny)
        return remote(send_rows.at[t], got.at[me], gs.at[t], gr.at[me], {"seq": t // ny, "index": lax.rem(t, ny)})

    def g_start(k, carry):
        g_copy(k).start()
        return carry

    lax.fori_loop(1, ns * ny, g_start, 0)
    got[me] = send_rows[me]

    for g in range(pieces):
        for here, there in edges:
            z_copy(g, here, there).wait_send()
    for d in (0,) + tuple(d for ds in order for d in ds):
        y_finish(d)
        if d:
            for which in range(2):
                x_copy(shifted(-d), which).wait_send()
                p_copy(shifted(-d), which).wait_send()
    for j in range(owned):
        for which in range(2):
            w_copy(j, which).wait_send()
            m_copy(j, which).wait_send()
    n_first().wait_send()
    for k in (1, 3):
        n_copy(k).wait_send()
        n_relay(k).wait_send()
    for pair in range(pairs):
        h_copy(pair).wait_send()
    for piece in range(2 * pairs):
        for k in (1, 3):
            c_copy(piece, k).wait_send()
            f_copy(piece, k).wait_send()
    for k in range(1, ns):
        i_copy(k).wait_send()

    def g_finish(k, carry):
        t = lax.rem(me + k, ns * ny)
        remote(send_rows.at[t], got.at[t], gs.at[t], gr.at[t], {"seq": t // ny, "index": lax.rem(t, ny)}).wait()
        return carry

    lax.fori_loop(1, ns * ny, g_finish, 0)
    parts = []
    for f in range(ny):
        part_sum = got[f]
        for t in range(1, ns):
            part_sum += got[t * ny + f]
        parts.append(part_sum)
    found = jnp.concatenate(parts, axis=1)
    mean = jnp.sum(found * found, axis=1, keepdims=True) / (quarter * ny)
    shelf_ref[...] = found * lax.rsqrt(mean + 1e-6)


def body(hidden, proj_weight, stretch_lengths, shard_of):
    states = hidden[0]
    tokens, depth = states.shape
    pieces, rows, width = proj_weight.shape
    nz, ns, ny = (lax.axis_size(a) for a in ("dp", "seq", "index"))
    pairs = width // 128
    quarter = depth // ny
    slots = shard_of.shape[1] // 2
    dma = pltpu.SemaphoreType.DMA
    bf16, f32 = jnp.bfloat16, jnp.float32
    any_space = pl.BlockSpec(memory_space=pl.ANY)
    vmem_space = pl.BlockSpec(memory_space=VMEM)
    layer, shelf = pl.pallas_call(
        layer_kernel,
        out_shape=(jax.ShapeDtypeStruct((tokens, quarter), bf16), jax.ShapeDtypeStruct((slots, depth), f32)),
        in_specs=[pl.BlockSpec(memory_space=pltpu.SMEM), vmem_space, any_space, any_space],
        out_specs=[vmem_space] * 2,
        scratch_shapes=[
            VMEM((tokens, depth), bf16), VMEM((tokens, depth), bf16),
            VMEM((nz, 3, rows, width), bf16),
            VMEM((nz, rows // 4, width), bf16),
            VMEM((ny, nz // ny, rows, width), bf16),
            VMEM((3, tokens, width), f32), VMEM((2, tokens, width), f32),
            VMEM((4, tokens, 128), f32),
            VMEM((pairs, tokens, 128), bf16),
            VMEM((pairs, 2, tokens, 128), bf16),
            VMEM((2, pairs, 2, tokens, 128), bf16),
            VMEM((ny, pairs, tokens, 128), bf16),
            VMEM((8, 128), jnp.int32), VMEM((ns, 8, 128), jnp.int32),
            VMEM((ns * 8, tokens), bf16),
            VMEM((ns * ny, slots, quarter), f32), VMEM((ns * ny, slots, quarter), f32),
            dma((2,)),
            dma((pieces, nz - 1)), dma((pieces, nz)),
            dma((2, nz)), dma((2, nz)), dma((2, nz)), dma((2, nz)),
            dma((nz,)), dma((ny, nz // ny)), dma((nz // ny,)),
            dma((2, nz // ny)), dma((2, nz // ny)), dma((2, nz // ny)), dma((2, nz // ny)),
            dma((7,)), dma((7,)),
            dma((pairs,)), dma((pairs,)),
            dma((2 * pairs, ny)), dma((2 * pairs, ny)), dma((2 * pairs, 2)), dma((2 * pairs, 2)),
            dma((ns,)), dma((ns,)), dma((ns * ny,)), dma((ns * ny,)),
        ],
        compiler_params=pltpu.CompilerParams(collective_id=0, has_side_effects=True),
    )(shard_of[0, :, 0], stretch_lengths, states, proj_weight)
    return (layer[None], shelf[None, None, None])


def solution(mesh):
    in_specs = (P("dp", "seq", None), P(None, "dp", "index"), P("dp", None), P("dp", "seq", None))
    out_specs = (P("dp", "seq", "index"), P("dp", "seq", "index", None, None))
    return jax.shard_map(body, mesh=mesh, in_specs=in_specs, out_specs=out_specs, check_vma=False)
```

```python
import jax
import jax.numpy as jnp
from jax import lax
from jax.experimental import pallas as pl
from jax.experimental.pallas import tpu as pltpu
from jax.sharding import PartitionSpec as P

HD = 64
MESH = pl.DeviceIdType.MESH
VMEM = pltpu.VMEM


def layer_kernel(shard_hbm, len_hbm, x_hbm, w_hbm, layer_ref, shelf_ref,
                 x_ref, near_x, w_all, w3_ring, w3, acc, near_acc, tables, queries, pair_kv, side, ctx,
                 shard_ref, len_ref, id_send, id_all, member, send_rows, got,
                 local, zs, zr, xs, xr, ps, pr, ys, yr, yl, ws, wr, ms, mr,
                 ns_, nr, hs, hr, cs, cr, fs, fr, is_, ir, gs, gr):
    nz = lax.axis_size("dp")
    ns = lax.axis_size("seq")
    ny = lax.axis_size("index")
    z = lax.axis_index("dp")
    s = lax.axis_index("seq")
    y = lax.axis_index("index")
    pieces, rows, width = w_hbm.shape
    tokens = x_ref.shape[0]
    pairs = width // 128
    quarter = layer_ref.shape[1]
    owned = nz // ny
    core = lax.rem(s, 2)
    par = lax.rem(s // 2, 2)
    mate = {"seq": s + 1 - 2 * core}
    right = {"seq": lax.rem(s + 2, ns)}
    left = {"seq": lax.rem(s + ns - 2, ns)}
    near = s + 2 * core - 1
    neighbour = {"seq": lax.rem(near + ns, ns)}
    me = s * ny + y
    count = len_hbm.shape[1]
    per_block = count // ns
    capacity = per_block // 2

    def remote(src, dst, send, recv, device):
        return pltpu.make_async_remote_copy(src_ref=src, dst_ref=dst, send_sem=send, recv_sem=recv,
                                            device_id=device, device_id_type=MESH)

    def shifted(d):
        return lax.rem(z + nz + d, nz)

    x_load = pltpu.make_async_copy(x_hbm, x_ref, local.at[0])
    shard_load = pltpu.make_async_copy(shard_hbm, shard_ref, local.at[2])
    shard_load.start()
    len_load = pltpu.make_async_copy(len_hbm, len_ref, local.at[3])
    len_load.start()
    x_load.start()
    own_load = pltpu.make_async_copy(w_hbm.at[pl.ds(0, 3)], w_all.at[z], local.at[1])
    own_load.start()

    barrier = pltpu.get_barrier_semaphore()
    far_first = sorted(((a, b) for a in range(ns) for b in range(ny) if a or b),
                       key=lambda p: -min(p[0] // 2, (ns - p[0]) // 2) - min(p[1], ny - p[1]))
    for a, b in far_first:
        pl.semaphore_signal(barrier, inc=1, device_id={"seq": lax.rem(s + a, ns), "index": lax.rem(y + b, ny)},
                            device_id_type=MESH)
    for d in (1, -1):
        pl.semaphore_signal(barrier, inc=1, device_id={"dp": shifted(d)}, device_id_type=MESH)
    shard_load.wait()
    len_load.wait()
    tile_row = lax.broadcasted_iota(jnp.int32, (8, 128), 0)
    ids = jnp.zeros((8, 128), jnp.int32)
    for i in range(per_block):
        ids = jnp.where(tile_row == i, shard_ref[i], ids)
    id_send[...] = ids
    id_all[s] = ids
    pl.semaphore_wait(barrier, ns * ny + 1)

    part = rows // 4
    sub = part // 2
    mine = pl.multiple_of(rows // 2 * par + part * core, 16)
    other = pl.multiple_of(rows // 2 * (1 - par) + part * core, 16)
    mate_mine = pl.multiple_of(rows // 2 * par + part * (1 - core), 16)
    mate_other = pl.multiple_of(rows // 2 * (1 - par) + part * (1 - core), 16)

    far = nz // 2
    edges = {}
    for d in range(far):
        for sign in ((1, -1) if d < far - 1 else (1,)):
            edges[sign * d, sign * (d + 1)] = len(edges)

    def z_ref(g, o):
        return w3_ring.at[o] if g == 3 else w_all.at[o, g, pl.ds(mine, part)]

    def z_copy(g, here, there):
        o = shifted(-here)
        dst = z_ref(g, o)
        src = w_hbm.at[g, pl.ds(mine, part)] if here == 0 else dst
        return remote(src, dst, zs.at[g, edges[here, there]], zr.at[g, o], {"dp": shifted(there - here)})

    def z_wait(g, d):
        o = shifted(-d)
        remote(z_ref(g, o), z_ref(g, o), zs.at[g, 0], zr.at[g, o], {"dp": shifted(1)}).wait_recv()

    def forward(g, d):
        for here, there in edges:
            if here == d:
                z_copy(g, here, there).start()

    def x_copy(o, which):
        ref = w_all.at[o, :, pl.ds(mine + which * sub, sub)]
        return remote(ref, ref, xs.at[which, o], xr.at[which, o], (right, left)[which])

    def x_wait(o, which):
        ref = w_all.at[o, :, pl.ds(other + which * sub, sub)]
        remote(ref, ref, xs.at[which, o], xr.at[which, o], right).wait_recv()

    def p_copy(o, which):
        ref = w_all.at[o, :, pl.ds((mine, other)[which], part)]
        return remote(ref, ref, ps.at[which, o], pr.at[which, o], mate)

    def p_wait(o, which):
        ref = w_all.at[o, :, pl.ds((mate_mine, mate_other)[which], part)]
        remote(ref, ref, ps.at[which, o], pr.at[which, o], mate).wait_recv()

    def y_local(d):
        o = shifted(-d)
        src = w_hbm.at[3, pl.ds(mine, part)] if d == 0 else w3_ring.at[o]
        j = lax.rem(o, owned)
        return pltpu.make_async_copy(src, w3.at[y, j, pl.ds(mine, part)], yl.at[j])

    def y_copy(d):
        o = shifted(-d)
        src = w_hbm.at[3, pl.ds(mine, part)] if d == 0 else w3_ring.at[o]
        j = lax.rem(o, owned)
        return remote(src, w3.at[y, j, pl.ds(mine, part)], ys.at[o], yr.at[y, j], {"index": o // owned})

    def y_start(d):
        stays = shifted(-d) // owned == y

        @pl.when(stays)
        def _():
            y_local(d).start()

        @pl.when(jnp.logical_not(stays))
        def _():
            y_copy(d).start()

    def y_finish(d):
        @pl.when(shifted(-d) // owned != y)
        def _():
            y_copy(d).wait_send()

    def w_copy(j, which):
        ref = w3.at[:, j, pl.ds(mine + which * sub, sub)]
        return remote(ref, ref, ws.at[which, j], wr.at[which, j], (right, left)[which])

    def w_wait(j, which):
        ref = w3.at[:, j, pl.ds(other + which * sub, sub)]
        remote(ref, ref, ws.at[which, j], wr.at[which, j], right).wait_recv()

    def m_copy(j, which):
        ref = w3.at[:, j, pl.ds((mine, other)[which], part)]
        return remote(ref, ref, ms.at[which, j], mr.at[which, j], mate)

    def m_wait(j, which):
        ref = w3.at[:, j, pl.ds((mate_mine, mate_other)[which], part)]
        remote(ref, ref, ms.at[which, j], mr.at[which, j], mate).wait_recv()

    def w_arrive(d):
        o = shifted(-d)
        j = lax.rem(o, owned)

        @pl.when(o // owned == y)
        def _():
            y_local(d).wait()
            for k in range(1, ny):
                f = lax.rem(y + k, ny)
                ref = w3.at[f, j, pl.ds(mine, part)]
                remote(ref, ref, ys.at[0], yr.at[f, j], {"index": f}).wait_recv()
            for which in range(2):
                w_copy(j, which).start()
            m_copy(j, 0).start()

    def w_cross(d):
        o = shifted(-d)
        j = lax.rem(o, owned)

        @pl.when(o // owned == y)
        def _():
            for which in range(2):
                w_wait(j, which)
            m_copy(j, 1).start()

    def beside(k):
        return {"index": lax.rem(y + k, ny)}

    share = tokens // ny

    def n_rows(k, lower_half=None):
        f = lax.rem(y + k, ny)
        if lower_half is None:
            return near_x.at[pl.ds(pl.multiple_of(f * share, share), share)]
        start = f * share + (0 if lower_half else share // 2)
        return near_x.at[pl.ds(pl.multiple_of(start, share // 2), share // 2)]

    def n_first():
        src = x_hbm.at[pl.ds(pl.multiple_of(y * share, share), share)]
        return remote(src, n_rows(0), ns_.at[0], nr.at[0], neighbour)

    def n_copy(k):
        return remote(n_rows(0), n_rows(0), ns_.at[k], nr.at[4 - k], beside(k))

    def n_wait(k):
        remote(n_rows(k), n_rows(k), ns_.at[k], nr.at[k], beside(k)).wait_recv()

    def n_relay(k):
        ref = n_rows(k, k == 3)
        return remote(ref, ref, ns_.at[3 + k], nr.at[3 + k], beside(ny - k))

    def n_relay_wait(k):
        ref = n_rows(2, k == 3)
        remote(ref, ref, ns_.at[3 + k], nr.at[3 + k], beside(k)).wait_recv()

    def i_copy(k):
        t = lax.rem(s + k, ns)
        return remote(id_send, id_all.at[s], is_.at[k], ir.at[s], {"seq": t})

    for g in range(pieces):
        forward(g, 0)
    y_start(0)
    n_first().start()
    for k in range(1, ns):
        i_copy(k).start()

    half = HD // 2
    lane = lax.broadcasted_iota(jnp.int32, (tokens, 128), 1)
    lower = lax.rem(lane, HD) < half
    freqs = jnp.exp(lax.rem(lane, half).astype(jnp.float32) * (-2.0 / HD * 9.210340371976184))
    token = lax.broadcasted_iota(jnp.int32, (tokens, 128), 0)

    def fill_tables(i, block):
        angles = (token + block * tokens).astype(jnp.float32) * freqs
        tables[2 * i] = jnp.cos(angles)
        sine = jnp.sin(angles)
        tables[2 * i + 1] = jnp.where(lower, -sine, sine)


    def arrive(ds):
        for d in ds:
            for g in range(3):
                z_wait(g, d)
                forward(g, d)
            for which in range(2):
                x_copy(shifted(-d), which).start()
            p_copy(shifted(-d), 0).start()
        for d in ds:
            z_wait(3, d)
            forward(3, d)
            y_start(d)

    def cross(ds):
        for d in ds:
            for which in range(2):
                x_wait(shifted(-d), which)
            p_copy(shifted(-d), 1).start()

    def lhs_of(ref, ds):
        return jnp.concatenate([ref[:, pl.ds(pl.multiple_of(o * rows, 128), rows)] for o in origins(ds)], axis=1)

    def origins(ds):
        return [shifted(-d) for d in (ds if len(ds) == 2 else (0, ds[0]))]

    def rhs_of(j, ds):
        return jnp.concatenate([w_all[o, j] for o in origins(ds)], axis=0)

    def near_multiply(ds, first):
        lhs = lhs_of(near_x, ds)
        for j in (1, 2):
            product = jnp.dot(lhs, rhs_of(j, ds), preferred_element_type=jnp.float32)
            near_acc[j - 1] = product if first else near_acc[j - 1] + product

    def settle(ds, first, both):
        for d in ds:
            for which in range(2):
                p_wait(shifted(-d), which)
        lhs = lhs_of(x_ref, ds)
        product = jnp.dot(lhs, rhs_of(0, ds), preferred_element_type=jnp.float32)
        acc[0] = product if first else acc[0] + product
        if both:
            lhs = jnp.concatenate([lhs, lhs_of(near_x, ds)], axis=0)
        for j in (1, 2):
            product = jnp.dot(lhs, rhs_of(j, ds), preferred_element_type=jnp.float32)
            acc[j] = product[:tokens] if first else acc[j] + product[:tokens]
            if both:
                near_acc[j - 1] += product[tokens:]

    def place_stretches():
        for k in range(1, ns):
            f = lax.rem(s + k, ns)
            remote(id_all.at[f], id_all.at[f], is_.at[k], ir.at[f], {"seq": f}).wait_recv()
        slots = ns * 8
        slot = lax.broadcasted_iota(jnp.int32, (slots, count), 0)
        stretch = lax.rem(slot, 8) * ns + slot // 8
        which_stretch = lax.broadcasted_iota(jnp.int32, (slots, count), 1)
        lengths = jnp.broadcast_to(len_ref[...], (slots, count))
        cube = (ns, 8, 128)

        def wide(picked):
            return jnp.broadcast_to(jnp.sum(jnp.where(picked, lengths, 0), axis=1, keepdims=True), (slots, 128)).reshape(cube)

        ends = wide(which_stretch <= stretch)
        starts = wide(which_stretch < stretch)
        line = lax.broadcasted_iota(jnp.int32, cube, 1)
        shard = id_all[...]

        def spread(value, i):
            return jnp.broadcast_to(value[:, i:i + 1, :], cube)

        rank = jnp.zeros(cube, jnp.int32)
        for i in range(per_block - 1):
            rank += jnp.where(jnp.logical_and(spread(shard, i) == shard, line > i), 1, 0)
        place = shard * capacity + rank
        first = jnp.zeros(cube, jnp.int32)
        last = jnp.zeros(cube, jnp.int32)
        for i in range(per_block):
            here = spread(place, i) == line
            first = jnp.where(here, spread(starts, i), first)
            last = jnp.where(here, spread(ends, i), last)
        first, last = first.reshape(slots, 128), last.reshape(slots, 128)
        for start in range(0, tokens, 128):
            position = lax.broadcasted_iota(jnp.int32, (slots, 128), 1) + (s * tokens + start)
            inside = jnp.logical_and(position >= first, position < last)
            member[:, start:start + 128] = jnp.where(inside, 1.0, 0.0).astype(jnp.bfloat16)

    order = [(d, -d) for d in range(1, far)] + [(far,)]
    turns = len(order) + 2
    for i in range(turns):
        if i < len(order):
            arrive(order[i])
        if 1 <= i <= len(order):
            cross(order[i - 1])
        if i == 1:
            n_first().wait_recv()
            for k in (1, 3):
                n_copy(k).start()
            x_load.wait()
            own_load.wait()
        if i == 2:
            place_stretches()
        if i == 3:
            fill_tables(0, s)
        if i == 4:
            for k in (1, 3):
                n_wait(k)
                n_relay(k).start()
        if i == 5:
            fill_tables(1, near)
        if i == 6:
            for k in (1, 3):
                n_relay_wait(k)
        if i in (6, 7):
            for m in (2 * i - 12, 2 * i - 11):
                near_multiply(order[m], m == 0)
        if i >= 2:
            settle(order[i - 2], i == 2, i >= 6)
        if i >= 4:
            for d in order[i - 4] + ((0,) if i == 4 else ()):
                w_arrive(d)
        if i >= 6:
            for d in order[i - 6] + ((0,) if i == 6 else ()):
                w_cross(d)

    def turned(value, i):
        swapped = jnp.where(lower, pltpu.roll(value, 128 - half, 1), pltpu.roll(value, half, 1))
        return value * tables[2 * i] + swapped * tables[2 * i + 1]

    def h_copy(pair):
        return remote(pair_kv.at[pair], side.at[core, pair], hs.at[pair], hr.at[pair], mate)

    def h_wait(pair):
        ref = side.at[1 - core, pair]
        remote(ref, ref, hs.at[pair], hr.at[pair], mate).wait_recv()

    blocks = [slice(pair * 128, pair * 128 + 128) for pair in range(pairs)]
    for pair, cols in enumerate(blocks):
        pair_kv[pair, 0] = turned(acc[1, :, cols], 0).astype(jnp.bfloat16)
        pair_kv[pair, 1] = acc[2, :, cols].astype(jnp.bfloat16)
        h_copy(pair).start()
    for pair, cols in enumerate(blocks):
        side[core, pair, 0] = turned(near_acc[0, :, cols], 1).astype(jnp.bfloat16)
        side[core, pair, 1] = near_acc[1, :, cols].astype(jnp.bfloat16)
        queries[pair] = (turned(acc[0, :, cols], 0) * HD ** -0.5).astype(jnp.bfloat16)

    for ds in order[turns - 4:]:
        for d in ds:
            w_arrive(d)

    strip = tokens // 2

    def c_rows(f, piece, start=0, size=strip):
        return ctx.at[f, piece // 2, pl.ds(piece % 2 * strip + start, size)]

    def c_copy(piece, k):
        ref = c_rows(y, piece)
        return remote(ref, ref, cs.at[piece, k], cr.at[piece, y], beside(k))

    def c_wait(piece, k):
        f = lax.rem(y + k, ny)
        ref = c_rows(f, piece)
        remote(ref, ref, cs.at[piece, k], cr.at[piece, f], beside(k)).wait_recv()

    def f_copy(piece, k):
        ref = c_rows(lax.rem(y + k, ny), piece, 0 if k == 3 else strip // 2, strip // 2)
        return remote(ref, ref, fs.at[piece, k // 2], fr.at[piece, k // 2], beside(ny - k))

    def f_wait(piece, k):
        ref = c_rows(lax.rem(y + 2, ny), piece, 0 if k == 3 else strip // 2, strip // 2)
        remote(ref, ref, fs.at[piece, k // 2], fr.at[piece, k // 2], beside(k)).wait_recv()

    def relay(piece):
        for k in (1, 3):
            c_wait(piece, k)
            f_copy(piece, k).start()

    def scores(query, key):
        return lax.dot_general(query, key, (((1,), (1,)), ((), ())), preferred_element_type=jnp.float32)

    lag = 4
    narrow = lax.broadcasted_iota(jnp.int32, (strip, 128), 1)
    for pair in range(pairs):
        h_wait(pair)
        for part_of in range(2):
            piece = 2 * pair + part_of
            top_row = part_of * strip
            query = queries[pair, top_row:top_row + strip]
            low_keys = slice(top_row, tokens)
            high_keys = slice(0, top_row + strip)
            low_shape = (strip, tokens - top_row)
            high_shape = (strip, top_row + strip)
            see_low = jnp.logical_and(lax.broadcasted_iota(jnp.int32, low_shape, 1) >= lax.broadcasted_iota(jnp.int32, low_shape, 0), s > 0)
            see_high = jnp.logical_and(
                lax.broadcasted_iota(jnp.int32, high_shape, 1) <= lax.broadcasted_iota(jnp.int32, high_shape, 0) + top_row, s < ns - 1)
            results = []
            for head in range(2):
                inside = (narrow < HD) if head == 0 else (narrow >= HD)
                chosen = jnp.where(inside, query, jnp.zeros_like(query))
                low = jnp.where(see_low, scores(chosen, side[0, pair, 0, low_keys]), -1e30)
                mid = scores(chosen, pair_kv[pair, 0])
                high = jnp.where(see_high, scores(chosen, side[1, pair, 0, high_keys]), -1e30)
                top = jnp.maximum(jnp.max(mid, axis=1, keepdims=True), jnp.maximum(
                    jnp.max(low, axis=1, keepdims=True), jnp.max(high, axis=1, keepdims=True)))
                low, mid, high = jnp.exp(low - top), jnp.exp(mid - top), jnp.exp(high - top)
                total = (jnp.sum(low, axis=1, keepdims=True) + jnp.sum(mid, axis=1, keepdims=True)
                         + jnp.sum(high, axis=1, keepdims=True))
                value = jnp.dot(low.astype(jnp.bfloat16), side[0, pair, 1, low_keys], preferred_element_type=jnp.float32)
                value += jnp.dot(mid.astype(jnp.bfloat16), pair_kv[pair, 1], preferred_element_type=jnp.float32)
                value += jnp.dot(high.astype(jnp.bfloat16), side[1, pair, 1, high_keys], preferred_element_type=jnp.float32)
                results.append(value / total)
            ctx[y, pair, top_row:top_row + strip] = jnp.where(narrow < HD, results[0], results[1]).astype(jnp.bfloat16)
            for k in (1, 3):
                c_copy(piece, k).start()
            if piece >= lag:
                relay(piece - lag)
            if piece == 2:
                for ds in order[turns - 6:]:
                    for d in ds:
                        w_cross(d)

    def project(k):
        f = lax.rem(y + k, ny)
        context = jnp.concatenate([ctx[f, pair] for pair in range(pairs)], axis=1)
        return jnp.concatenate([scores(context, w3[f, j]) for j in range(owned)], axis=1)

    for j in range(owned):
        for which in range(2):
            m_wait(j, which)
    summed = x_ref[:, pl.ds(pl.multiple_of(y * quarter, 128), quarter)].astype(jnp.float32) + project(0)
    for piece in range(2 * pairs - lag, 2 * pairs):
        relay(piece)
    summed += project(1)
    summed += project(3)
    for piece in range(2 * pairs):
        for k in (1, 3):
            f_wait(piece, k)
    summed += project(2)
    layer = summed.astype(jnp.bfloat16)
    layer_ref[...] = layer

    partial = jnp.dot(member[...], layer, preferred_element_type=jnp.float32)
    for t in range(ns * ny):
        send_rows[t] = partial[t * capacity:(t + 1) * capacity]

    def g_copy(k):
        t = lax.rem(me + k, ns * ny)
        return remote(send_rows.at[t], got.at[me], gs.at[t], gr.at[me], {"seq": t // ny, "index": lax.rem(t, ny)})

    def g_start(k, carry):
        g_copy(k).start()
        return carry

    lax.fori_loop(1, ns * ny, g_start, 0)
    got[me] = send_rows[me]

    for g in range(pieces):
        for here, there in edges:
            z_copy(g, here, there).wait_send()
    for d in (0,) + tuple(d for ds in order for d in ds):
        y_finish(d)
        if d:
            for which in range(2):
                x_copy(shifted(-d), which).wait_send()
                p_copy(shifted(-d), which).wait_send()
    for j in range(owned):
        for which in range(2):
            w_copy(j, which).wait_send()
            m_copy(j, which).wait_send()
    n_first().wait_send()
    for k in (1, 3):
        n_copy(k).wait_send()
        n_relay(k).wait_send()
    for pair in range(pairs):
        h_copy(pair).wait_send()
    for piece in range(2 * pairs):
        for k in (1, 3):
            c_copy(piece, k).wait_send()
            f_copy(piece, k).wait_send()
    for k in range(1, ns):
        i_copy(k).wait_send()

    def g_finish(k, carry):
        t = lax.rem(me + k, ns * ny)
        remote(send_rows.at[t], got.at[t], gs.at[t], gr.at[t], {"seq": t // ny, "index": lax.rem(t, ny)}).wait()
        return carry

    lax.fori_loop(1, ns * ny, g_finish, 0)
    parts = []
    for f in range(ny):
        part_sum = got[f]
        for t in range(1, ns):
            part_sum += got[t * ny + f]
        parts.append(part_sum)
    found = jnp.concatenate(parts, axis=1)
    mean = jnp.sum(found * found, axis=1, keepdims=True) / (quarter * ny)
    shelf_ref[...] = found * lax.rsqrt(mean + 1e-6)


def body(hidden, proj_weight, stretch_lengths, shard_of):
    states = hidden[0]
    tokens, depth = states.shape
    pieces, rows, width = proj_weight.shape
    nz, ns, ny = (lax.axis_size(a) for a in ("dp", "seq", "index"))
    pairs = width // 128
    quarter = depth // ny
    slots = shard_of.shape[1] // 2
    dma = pltpu.SemaphoreType.DMA
    bf16, f32 = jnp.bfloat16, jnp.float32
    any_space = pl.BlockSpec(memory_space=pl.ANY)
    vmem_space = pl.BlockSpec(memory_space=VMEM)
    layer, shelf = pl.pallas_call(
        layer_kernel,
        out_shape=(jax.ShapeDtypeStruct((tokens, quarter), bf16), jax.ShapeDtypeStruct((slots, depth), f32)),
        in_specs=[any_space] * 4,
        out_specs=[vmem_space] * 2,
        scratch_shapes=[
            VMEM((tokens, depth), bf16), VMEM((tokens, depth), bf16),
            VMEM((nz, 3, rows, width), bf16),
            VMEM((nz, rows // 4, width), bf16),
            VMEM((ny, nz // ny, rows, width), bf16),
            VMEM((3, tokens, width), f32), VMEM((2, tokens, width), f32),
            VMEM((4, tokens, 128), f32),
            VMEM((pairs, tokens, 128), bf16),
            VMEM((pairs, 2, tokens, 128), bf16),
            VMEM((2, pairs, 2, tokens, 128), bf16),
            VMEM((ny, pairs, tokens, 128), bf16),
            pltpu.SMEM((shard_of.shape[1],), jnp.int32), VMEM((1, stretch_lengths.shape[1]), jnp.int32),
            VMEM((8, 128), jnp.int32), VMEM((ns, 8, 128), jnp.int32),
            VMEM((ns * 8, tokens), bf16),
            VMEM((ns * ny, slots, quarter), f32), VMEM((ns * ny, slots, quarter), f32),
            dma((4,)),
            dma((pieces, nz - 1)), dma((pieces, nz)),
            dma((2, nz)), dma((2, nz)), dma((2, nz)), dma((2, nz)),
            dma((nz,)), dma((ny, nz // ny)), dma((nz // ny,)),
            dma((2, nz // ny)), dma((2, nz // ny)), dma((2, nz // ny)), dma((2, nz // ny)),
            dma((7,)), dma((7,)),
            dma((pairs,)), dma((pairs,)),
            dma((2 * pairs, ny)), dma((2 * pairs, ny)), dma((2 * pairs, 2)), dma((2 * pairs, 2)),
            dma((ns,)), dma((ns,)), dma((ns * ny,)), dma((ns * ny,)),
        ],
        compiler_params=pltpu.CompilerParams(collective_id=0, has_side_effects=True),
    )(shard_of[0, :, 0], stretch_lengths, states, proj_weight)
    return (layer[None], shelf[None, None, None])


def solution(mesh):
    in_specs = (P("dp", "seq", None), P(None, "dp", "index"), P("dp", None), P("dp", "seq", None))
    out_specs = (P("dp", "seq", "index"), P("dp", "seq", "index", None, None))
    return jax.shard_map(body, mesh=mesh, in_specs=in_specs, out_specs=out_specs, check_vma=False)
```
